128 devices in a mesh: tgt: 32 (over z_hi, y, x), grp: 4 (over z_lo, core).
Axes of the slice: x: 4, y: 4, z: 4 (z_hi: 2, z_lo: 2; z = z_hi * 2 + z_lo), core: 2. Of those that a mesh axis runs over, the one named last changes fastest.
Arguments:
- targets: bfloat16 [32, 64, 64, 128], P('tgt', 'grp'), may hold values from -6 to 6
- partners: bfloat16 [32, 64, 64, 128], P('tgt'), may hold values from -6 to 6
- occupations: float32 [32], replicated, may hold values from 0.2 to 2
- slot_partner: int32 [32], replicated, may hold values from 0 to 31, each once
- screening: float32 [1], replicated, may hold values from 0.3 to 0.6
Outputs:
- exchange: float32 [32, 64, 64, 128], P('tgt', 'grp')
The draws below stay inside these ranges and needn't reach their ends.
Inputs may be any that keep to these rules, and one draw needn't show every extreme that they name: `slot_partner`: every partner id appears in exactly one slot.
All inputs are finite; a program needn't handle non-finite values.
Results may differ from the reference program's by a relative error of at most 0.011.
Values may be sent and summed in bfloat16 or wider, within the bound.
No kernel may reach another device: no remote copies, remote signals or barrier semaphores. Data moves between devices by JAX's collectives and lax.ppermute only.
A program may use at most 64 MiB of HBM per device.

```python
import math
import jax
import jax.numpy as jnp
from jax import lax

NG = 64
NT = 32
NPART = 32


def level_of(own_key, extent, pieces, low, largest):
    level = 1.0
    for dim, parts in pieces:
        heights = jax.random.uniform(jax.random.fold_in(jax.random.fold_in(own_key, 6), dim), (parts,), jnp.float32, low / len(pieces), largest / len(pieces))
        level = level * jnp.repeat(jnp.exp(heights), extent[dim] // parts).reshape((-1,) + (1,) * (len(extent) - 1 - dim))
    return level


def noise(own_key, shape, scale, limit, shards=(), kind=jnp.bfloat16):
    gain = level_of(own_key, shape, shards, -0.22, 0.18) if shards else 1.0
    drawn = jax.random.normal(own_key, shape, jnp.float32) * scale * gain
    return jnp.minimum(jnp.maximum(drawn, -limit), limit).astype(kind)


def setup_inputs(seed: int = 0) -> dict:
    key_list = jax.random.split(jax.random.key(seed), 6)
    targets = noise(key_list[0], (NT, NG, NG, 2 * NG), 1.0, 6.0, ((0, 32), (1, 4)))
    partners = noise(key_list[1], (NPART, NG, NG, 2 * NG), 1.0, 6.0, ((0, 32),))
    occupations = jnp.clip(jnp.exp(jax.random.uniform(key_list[2], (NPART,), jnp.float32, math.log(0.2), math.log(2.0))), 0.2, 2.0)
    slot_partner = jax.random.permutation(key_list[3], NPART).astype(jnp.int32)
    screening = jnp.clip(jnp.exp(jax.random.uniform(key_list[4], (1,), jnp.float32, math.log(0.3), math.log(0.6))), 0.3, 0.6)
    return {"targets": targets, "partners": partners, "occupations": occupations, "slot_partner": slot_partner, "screening": screening}


coulomb_scale = 0.1

def fourier_table(points):
    indices = jnp.arange(points, dtype=jnp.int32)
    phases = indices[:, None] * indices[None, :] % points
    angles = phases.astype(jnp.float32) * (2.0 * math.pi / points)
    norm_factor = 1.0 / math.sqrt(points)
    return jnp.concatenate([jnp.cos(angles) * norm_factor, jnp.sin(angles) * norm_factor], axis=0).astype(jnp.bfloat16)

def coulomb_kernel(points, screening):
    indices = jnp.arange(points, dtype=jnp.int32)
    signed = jnp.where(indices < points // 2, indices, indices - points).astype(jnp.float32) * (2.0 * math.pi / points)
    squares = signed * signed
    wave_sq = squares[:, None, None] + squares[None, :, None] + squares[None, None, :]
    screen_wave = screening[0] * (2.0 * math.pi / points)
    inverse_sq = coulomb_scale / (wave_sq + screen_wave * screen_wave)
    return jnp.concatenate([inverse_sq, inverse_sq], axis=-1)

def slot_weights(occupations, slot_partner):
    ids = jnp.arange(occupations.shape[0], dtype=jnp.int32)
    match = slot_partner[:, None] == ids[None, :]
    return lax.optimization_barrier(jnp.sum(jnp.where(match, occupations[None, :], 0.0), axis=1))

def last_axis_matrix(tables, orient):
    points = tables.shape[1]
    cosine = tables[:points].T
    sine_part = tables[points:].T
    upper_rows = jnp.concatenate([cosine, -orient * sine_part], axis=1)
    bottom = jnp.concatenate([orient * sine_part, cosine], axis=1)
    return jnp.concatenate([upper_rows, bottom], axis=0)

def combine(cos_part, sin_part, orient, points):
    real_part = cos_part[..., :points] + orient * sin_part[..., points:]
    imag_part = cos_part[..., points:] - orient * sin_part[..., :points]
    return jnp.concatenate([real_part, imag_part], axis=-1).astype(jnp.bfloat16)

def section_last(field, tables, orient):
    points = tables.shape[1]
    field = lax.optimization_barrier(field)
    matrix = last_axis_matrix(tables, orient).astype(jnp.float32)
    flat = field.reshape(-1, 2 * points).astype(jnp.float32)
    result = jnp.dot(flat, matrix, precision=lax.Precision.HIGHEST, preferred_element_type=jnp.float32)
    return result.reshape(field.shape).astype(jnp.bfloat16)

def section_middle(field, tables, orient):
    points = tables.shape[1]
    field = lax.optimization_barrier(field)
    stacked = jnp.einsum('ky,bxyw->bxkw', tables.astype(jnp.float32), field.astype(jnp.float32), precision=lax.Precision.HIGHEST)
    return combine(stacked[:, :, :points], stacked[:, :, points:], orient, points)

def section_first(field, tables, orient):
    points = tables.shape[1]
    field = lax.optimization_barrier(field)
    stacked = jnp.einsum('kx,bxyw->bkyw', tables.astype(jnp.float32), field.astype(jnp.float32), precision=lax.Precision.HIGHEST)
    return combine(stacked[:, :points], stacked[:, points:], orient, points)

def exchange_term(targets, partner, weight, tables, kernel):
    points = tables.shape[1]
    part_real = partner[..., :points].astype(jnp.float32)
    part_imag = partner[..., points:].astype(jnp.float32)
    tgt_real = targets[..., :points].astype(jnp.float32)
    tgt_imag = targets[..., points:].astype(jnp.float32)
    density = jnp.concatenate([part_real * tgt_real + part_imag * tgt_imag, part_real * tgt_imag - part_imag * tgt_real], axis=-1).astype(jnp.bfloat16)
    spectrum = section_first(section_middle(section_last(density, tables, 1.0), tables, 1.0), tables, 1.0)
    spectrum = lax.optimization_barrier(spectrum)
    scaled = (spectrum.astype(jnp.float32) * kernel).astype(jnp.bfloat16)
    potential = section_last(section_middle(section_first(scaled, tables, -1.0), tables, -1.0), tables, -1.0)
    potential = lax.optimization_barrier(potential)
    pot_real = potential[..., :points].astype(jnp.float32)
    pot_imag = potential[..., points:].astype(jnp.float32)
    real_part = pot_real * part_real - pot_imag * part_imag
    imag_part = pot_real * part_imag + pot_imag * part_real
    return weight * jnp.concatenate([real_part, imag_part], axis=-1)

def reference(targets, partners, occupations, slot_partner, screening):
    points = targets.shape[1]
    tables = fourier_table(points)
    kernel = coulomb_kernel(points, screening)
    slot_weight = slot_weights(occupations, slot_partner)

    def advance(totals, inputs):
        partner, weight = inputs
        return (totals + exchange_term(targets, partner, weight, tables, kernel), None)
    totals, _ = lax.scan(advance, jnp.zeros(targets.shape, jnp.float32), (partners, slot_weight))
    return -totals
```

```python
import functools
import math

import jax
import jax.numpy as jnp
import numpy as np
from jax import lax
from jax.experimental import pallas as pl
from jax.experimental.pallas import tpu as pltpu
from jax.sharding import PartitionSpec as P

coulomb_scale = 0.1
points = 64
lanes = 2 * points
quarter = 16
pitch = 72
axes = ("tgt", "grp")
f32 = jnp.float32
bf16 = jnp.bfloat16


devices = [
    (zh, y, x, zl, c)
    for zh in range(2)
    for y in range(4)
    for x in range(4)
    for zl in range(2)
    for c in range(2)
]
number = {device: i for i, device in enumerate(devices)}


def outer(i):
    return (i + 3) % 4 if i % 2 == 0 else (i + 1) % 4


def first_source(zh, y, x, zl, c):
    return {
        (0, 0): (zh, y, x, 0, 1),
        (0, 1): (zh ^ 1, y, x, 1, 0),
        (1, 0): (zh, outer(y), x, 1, 1),
        (1, 1): (zh ^ 1, y, outer(x), 0, 0),
    }[zl, c]


def second_source(zh, y, x, zl, c):
    return {
        (0, 0): (zh, outer(y), outer(x), 0, 0),
        (0, 1): (zh ^ 1, outer(y), outer(x), 1, 0),
        (1, 0): (zh, y, outer(x), 1, 1),
        (1, 1): (zh ^ 1, outer(y), x, 0, 1),
    }[zl, c]


def offset_source(dy, dx, dz, dc):
    return lambda zh, y, x, zl, c: (zh, y ^ dy, x ^ dx, zl ^ dz, c ^ dc)


def receive(value, source):
    pairs = [(number[source(*device)], number[device]) for device in devices]
    return lax.ppermute(value, axes, pairs)


def slot_table():
    slot = lambda d: (d[0] * 4 + d[1]) * 4 + d[2]
    return np.array(
        [[slot(first_source(*d)), slot(second_source(*d))] for d in devices], np.int32
    )


def tables():
    indices = np.arange(points)
    phases = indices[:, None] * indices[None, :] % points
    angles = phases.astype(np.float32) * np.float32(2.0 * math.pi / points)
    scale = np.float32(1.0 / math.sqrt(points))
    rounded = lambda t: (t * scale).astype(bf16).astype(np.float32)
    return rounded(np.cos(angles)), rounded(np.sin(angles))


def section_matrices():
    cosine, sine = tables()
    both = lambda t: np.kron(np.eye(2, dtype=np.float32), t)
    left_forward = np.block([[cosine, sine], [-sine, cosine]])
    left_inverse = np.block([[cosine, -sine], [sine, cosine]])
    right_forward = np.block([[both(cosine), both(-sine)], [both(sine), both(cosine)]])
    right_inverse = np.block([[both(cosine), both(sine)], [both(-sine), both(cosine)]])
    return [
        jnp.asarray(m, bf16) for m in (left_forward, left_inverse, right_forward, right_inverse)
    ]


def coulomb_kernel(screening):
    indices = jnp.arange(points, dtype=jnp.int32)
    signed = jnp.where(indices < points // 2, indices, indices - points).astype(f32) * (
        2.0 * math.pi / points
    )
    squares = signed * signed
    wave_sq = squares[:, None, None] + squares[None, :, None] + jnp.tile(squares, 2)[None, None, :]
    screen_wave = screening[0] * (2.0 * math.pi / points)
    return coulomb_scale / (wave_sq + screen_wave * screen_wave)


def pair_kernel(
    place_ref, occupations_ref, slot_partner_ref,
    t0, t1, t2, t3, pa, pb, coulomb, lf_ref, li_ref, rf_ref, ri_ref,
    out,
    t_v, a_v, b_v, k_v, s_ref, o_v, in_sem, k_sem, out_sem,
):
    dot = functools.partial(jnp.dot, preferred_element_type=f32)
    place = place_ref[0]
    rows = quarter * points
    low = lax.broadcasted_iota(jnp.int32, (rows, lanes), 1) < points

    def block_of(step):
        return place ^ (2 * (step // 2) + step % 2)

    def fetches(step, t_ref):
        planes = pl.ds(block_of(step) * quarter, quarter)
        return [
            pltpu.make_async_copy(t_ref, t_v.at[step], in_sem.at[step, 0]),
            pltpu.make_async_copy(pa.at[planes], a_v.at[step], in_sem.at[step, 1]),
            pltpu.make_async_copy(pb.at[planes], b_v.at[step], in_sem.at[step, 2]),
        ]

    for step, t_ref in enumerate((t0, t1, t2, t3)):
        for copy in fetches(step, t_ref):
            copy.start()
    k_copy = pltpu.make_async_copy(coulomb, k_v, k_sem)
    k_copy.start()
    lf = lf_ref[...]
    li = li_ref[...]

    def load(ref, step):
        return ref[step].reshape(rows, lanes).astype(f32)

    def partner_parts(step):
        a = load(a_v, step)
        b = load(b_v, step)
        real = jnp.where(low, a, pltpu.roll(b, points, 1))
        imag = jnp.where(low, pltpu.roll(a, points, 1), b)
        return real, imag

    def forward(step, carry):
        for copy in fetches(step, t0):
            copy.wait()
        plane = block_of(step) * quarter
        t = load(t_v, step)
        swapped = pltpu.roll(t, points, 1)
        t_real = jnp.where(low, t, swapped)
        t_imag = jnp.where(low, swapped, t)
        p_real, p_imag = partner_parts(step)
        density = jnp.concatenate(
            [
                (p_real * t_real + p_imag * t_imag).astype(bf16),
                (p_real * t_imag - p_imag * t_real).astype(bf16),
            ],
            axis=1,
        )
        along_z = dot(density, rf_ref[...]).astype(bf16)
        columns = []
        for j in range(quarter):
            part = along_z[j * points : (j + 1) * points]
            columns.append(jnp.concatenate([part[:, :lanes], part[:, lanes:]], axis=0))
        along_y = dot(lf, jnp.concatenate(columns, axis=1))
        for j in range(quarter):
            s_ref[pl.ds(plane + j, lanes, stride=pitch), :] = along_y[:, j * lanes : (j + 1) * lanes]
        return carry

    lax.fori_loop(0, 4, forward, 0)
    k_copy.wait()

    def line(k, part):
        return pl.ds(pl.multiple_of((part * points + k) * pitch, 8), points)

    def middle(i, carry):
        first = i * quarter
        columns = []
        for j in range(quarter):
            parts = [s_ref[line(first + j, part), :].astype(bf16) for part in range(2)]
            columns.append(jnp.concatenate(parts, axis=0))
        spectrum = dot(lf, jnp.concatenate(columns, axis=1))
        weights = jnp.concatenate([k_v[first + j] for j in range(quarter)], axis=1)
        scaled = (spectrum * jnp.concatenate([weights, weights], axis=0)).astype(bf16)
        along_x = dot(li, scaled)
        for j in range(quarter):
            for part in range(2):
                s_ref[line(first + j, part), :] = along_x[
                    part * points : (part + 1) * points, j * lanes : (j + 1) * lanes
                ]
        return carry

    lax.fori_loop(0, 4, middle, 0)
    weight = [occupations_ref[slot_partner_ref[place_ref[1 + i]]] for i in range(2)]
    weight = jnp.where(low, weight[0], weight[1])

    def put(step):
        return pltpu.make_async_copy(o_v.at[step], out.at[step], out_sem.at[step])

    def inverse(step, carry):
        plane = block_of(step) * quarter
        columns = [
            s_ref[pl.ds(plane + j, lanes, stride=pitch), :].astype(bf16) for j in range(quarter)
        ]
        along_y = dot(li, jnp.concatenate(columns, axis=1)).astype(bf16)
        field = []
        for j in range(quarter):
            part = along_y[:, j * lanes : (j + 1) * lanes]
            field.append(jnp.concatenate([part[:points], part[points:]], axis=1))
        potential = dot(jnp.concatenate(field, axis=0), ri_ref[...])
        v_real = potential[:, :lanes] * weight
        v_imag = potential[:, lanes:] * weight
        p_real, p_imag = partner_parts(step)
        real = v_real * p_real - v_imag * p_imag
        imag = v_real * p_imag + v_imag * p_real
        total = jnp.where(low, real, imag) + pltpu.roll(jnp.where(low, imag, real), points, 1)
        o_v[step] = total.astype(bf16).reshape(quarter, points, lanes)
        put(step).start()
        return carry

    lax.fori_loop(0, 4, inverse, 0)
    for step in range(4):
        put(step).wait()


def exchange_part(place, occupations, slot_partner, pieces, first, second, coulomb, matrices):
    anywhere = pl.BlockSpec(memory_space=pl.ANY)
    scalar = pl.BlockSpec(memory_space=pltpu.SMEM)
    near = pl.BlockSpec(memory_space=pltpu.VMEM)
    planes = (4, quarter, points, lanes)
    return pl.pallas_call(
        pair_kernel,
        out_shape=jax.ShapeDtypeStruct(planes, bf16),
        in_specs=[scalar] * 3 + [anywhere] * 7 + [near] * 4,
        out_specs=anywhere,
        scratch_shapes=[
            pltpu.VMEM(planes, bf16),
            pltpu.VMEM(planes, bf16),
            pltpu.VMEM(planes, bf16),
            pltpu.VMEM((points, points, lanes), f32),
            pltpu.VMEM((2 * points * pitch, lanes), f32),
            pltpu.VMEM(planes, bf16),
            pltpu.SemaphoreType.DMA((4, 3)),
            pltpu.SemaphoreType.DMA,
            pltpu.SemaphoreType.DMA((4,)),
        ],
        compiler_params=pltpu.CompilerParams(vmem_limit_bytes=40 << 20),
        cost_estimate=pl.CostEstimate(
            flops=5 * 10**9, bytes_accessed=24 * 2**20, transcendentals=0
        ),
    )(place, occupations, slot_partner, *pieces, first, second, coulomb, *matrices)


def body(targets, partners, occupations, slot_partner, screening):
    own = targets[0]
    partner = partners[0]
    first = receive(partner, first_source)
    second = receive(partner, second_source)
    orders = [(0, 1), (1, 0), (1, 1), (0, 0)]
    halves = []
    for dy, dx in orders:
        same = own if (dy, dx) == (0, 0) else receive(own, offset_source(dy, dx, 0, 0))
        halves.append((same, receive(own, offset_source(dy, dx, 1, 0))))
    coulomb = coulomb_kernel(screening)
    matrices = section_matrices()
    device = lax.axis_index("tgt") * 4 + lax.axis_index("grp")
    slots = lax.dynamic_slice_in_dim(jnp.asarray(slot_table()), device, 1)[0]
    place = jnp.concatenate([lax.axis_index("grp")[None].astype(jnp.int32), slots])
    sibling = offset_source(0, 0, 0, 1)
    terms = []
    for (dy, dx), (same, other) in zip(orders, halves):
        pieces = [same, receive(same, sibling), other, receive(other, sibling)]
        part = exchange_part(
            place, occupations, slot_partner, pieces, first, second, coulomb, matrices
        )
        for dz in range(2):
            crossed = receive(part[2 * dz + 1], sibling)
            summed = part[2 * dz].astype(f32) + crossed.astype(f32)
            if (dy, dx, dz) != (0, 0, 0):
                summed = receive(summed.astype(bf16), offset_source(dy, dx, dz, 0)).astype(f32)
            terms.append(summed)
    return -sum(terms[1:], terms[0])[None]


def solution(mesh):
    in_specs = (P("tgt", "grp", None, None), P("tgt", None, None, None), P(), P(), P())
    out_specs = P("tgt", "grp", None, None)
    return jax.shard_map(body, mesh=mesh, in_specs=in_specs, out_specs=out_specs, check_vma=False)
```

```python
import functools
import math

import jax
import jax.numpy as jnp
import numpy as np
from jax import lax
from jax.experimental import pallas as pl
from jax.experimental.pallas import tpu as pltpu
from jax.sharding import PartitionSpec as P


coulomb_scale = 0.1
points = 64
lanes = 2 * points
quarter = 16
pitch = 72
axes = ("tgt", "grp")
f32 = jnp.float32
bf16 = jnp.bfloat16


devices = [
    (zh, y, x, zl, c)
    for zh in range(2)
    for y in range(4)
    for x in range(4)
    for zl in range(2)
    for c in range(2)
]
number = {device: i for i, device in enumerate(devices)}


def outer(i):
    return (i + 3) % 4 if i % 2 == 0 else (i + 1) % 4


def first_source(zh, y, x, zl, c):
    return {
        (0, 0): (zh, y, x, 0, 1),
        (0, 1): (zh ^ 1, y, x, 1, 0),
        (1, 0): (zh, outer(y), x, 1, 1),
        (1, 1): (zh ^ 1, y, outer(x), 0, 0),
    }[zl, c]


def second_source(zh, y, x, zl, c):
    return {
        (0, 0): (zh, outer(y), outer(x), 0, 1),
        (0, 1): (zh ^ 1, outer(y), outer(x), 1, 0),
        (1, 0): (zh, y, outer(x), 1, 1),
        (1, 1): (zh ^ 1, outer(y), x, 0, 0),
    }[zl, c]


def offset_source(dy, dx, dz, dc):
    return lambda zh, y, x, zl, c: (zh, y ^ dy, x ^ dx, zl ^ dz, c ^ dc)


def receive(value, source):
    pairs = [(number[source(*device)], number[device]) for device in devices]
    return lax.ppermute(value, axes, pairs)


def slot_table():
    slot = lambda d: (d[0] * 4 + d[1]) * 4 + d[2]
    return np.array(
        [[slot(first_source(*d)), slot(second_source(*d))] for d in devices], np.int32
    )


def tables():
    indices = np.arange(points)
    phases = indices[:, None] * indices[None, :] % points
    angles = phases.astype(np.float32) * np.float32(2.0 * math.pi / points)
    scale = np.float32(1.0 / math.sqrt(points))
    rounded = lambda t: (t * scale).astype(bf16).astype(np.float32)
    return rounded(np.cos(angles)), rounded(np.sin(angles))


def section_matrices():
    cosine, sine = tables()
    both = lambda t: np.kron(np.eye(2, dtype=np.float32), t)
    left_forward = np.block([[cosine, sine], [-sine, cosine]])
    left_inverse = np.block([[cosine, -sine], [sine, cosine]])
    right_forward = np.block([[both(cosine), both(-sine)], [both(sine), both(cosine)]])
    right_inverse = np.block([[both(cosine), both(sine)], [both(-sine), both(cosine)]])
    return [
        jnp.asarray(m, bf16) for m in (left_forward, left_inverse, right_forward, right_inverse)
    ]


def coulomb_kernel(screening):
    indices = jnp.arange(points, dtype=jnp.int32)
    signed = jnp.where(indices < points // 2, indices, indices - points).astype(f32) * (
        2.0 * math.pi / points
    )
    squares = signed * signed
    wave_sq = squares[:, None, None] + squares[None, :, None] + jnp.tile(squares, 2)[None, None, :]
    screen_wave = screening[0] * (2.0 * math.pi / points)
    return coulomb_scale / (wave_sq + screen_wave * screen_wave)


def pair_kernel(
    place_ref, occupations_ref, slot_partner_ref,
    t0, t1, t2, t3, pa, pb, coulomb, lf_ref, li_ref, rf_ref, ri_ref,
    out,
    t_v, a_v, b_v, k_v, s_ref, o_v, in_sem, k_sem, out_sem,
):
    dot = functools.partial(jnp.dot, preferred_element_type=f32)
    place = place_ref[0]
    rows = quarter * points
    low = lax.broadcasted_iota(jnp.int32, (rows, lanes), 1) < points

    def block_of(step):
        return place ^ (2 * (step // 2) + step % 2)

    def fetches(step, t_ref):
        planes = pl.ds(block_of(step) * quarter, quarter)
        return [
            pltpu.make_async_copy(t_ref, t_v.at[step], in_sem.at[step, 0]),
            pltpu.make_async_copy(pa.at[planes], a_v.at[step], in_sem.at[step, 1]),
            pltpu.make_async_copy(pb.at[planes], b_v.at[step], in_sem.at[step, 2]),
        ]

    for step, t_ref in enumerate((t0, t1, t2, t3)):
        for copy in fetches(step, t_ref):
            copy.start()
    k_copy = pltpu.make_async_copy(coulomb, k_v, k_sem)
    k_copy.start()
    lf = lf_ref[...]
    li = li_ref[...]

    def load(ref, step):
        return ref[step].reshape(rows, lanes).astype(f32)

    def partner_parts(step):
        a = load(a_v, step)
        b = load(b_v, step)
        real = jnp.where(low, a, pltpu.roll(b, points, 1))
        imag = jnp.where(low, pltpu.roll(a, points, 1), b)
        return real, imag

    def forward(step, carry):
        for copy in fetches(step, t0):
            copy.wait()
        plane = block_of(step) * quarter
        t = load(t_v, step)
        swapped = pltpu.roll(t, points, 1)
        t_real = jnp.where(low, t, swapped)
        t_imag = jnp.where(low, swapped, t)
        p_real, p_imag = partner_parts(step)
        density = jnp.concatenate(
            [
                (p_real * t_real + p_imag * t_imag).astype(bf16),
                (p_real * t_imag - p_imag * t_real).astype(bf16),
            ],
            axis=1,
        )
        along_z = dot(density, rf_ref[...]).astype(bf16)
        columns = []
        for j in range(quarter):
            part = along_z[j * points : (j + 1) * points]
            columns.append(jnp.concatenate([part[:, :lanes], part[:, lanes:]], axis=0))
        along_y = dot(lf, jnp.concatenate(columns, axis=1))
        for j in range(quarter):
            s_ref[pl.ds(plane + j, lanes, stride=pitch), :] = along_y[:, j * lanes : (j + 1) * lanes]
        return carry

    lax.fori_loop(0, 4, forward, 0)
    k_copy.wait()

    def line(k, part):
        return pl.ds(pl.multiple_of((part * points + k) * pitch, 8), points)

    def middle(i, carry):
        first = i * quarter
        columns = []
        for j in range(quarter):
            parts = [s_ref[line(first + j, part), :].astype(bf16) for part in range(2)]
            columns.append(jnp.concatenate(parts, axis=0))
        spectrum = dot(lf, jnp.concatenate(columns, axis=1))
        weights = jnp.concatenate([k_v[first + j] for j in range(quarter)], axis=1)
        scaled = (spectrum * jnp.concatenate([weights, weights], axis=0)).astype(bf16)
        along_x = dot(li, scaled)
        for j in range(quarter):
            for part in range(2):
                s_ref[line(first + j, part), :] = along_x[
                    part * points : (part + 1) * points, j * lanes : (j + 1) * lanes
                ]
        return carry

    lax.fori_loop(0, 4, middle, 0)
    weight = [occupations_ref[slot_partner_ref[place_ref[1 + i]]] for i in range(2)]
    weight = jnp.where(low, weight[0], weight[1])

    def put(step):
        return pltpu.make_async_copy(o_v.at[step], out.at[step], out_sem.at[step])

    def inverse(step, carry):
        plane = block_of(step) * quarter
        columns = [
            s_ref[pl.ds(plane + j, lanes, stride=pitch), :].astype(bf16) for j in range(quarter)
        ]
        along_y = dot(li, jnp.concatenate(columns, axis=1)).astype(bf16)
        field = []
        for j in range(quarter):
            part = along_y[:, j * lanes : (j + 1) * lanes]
            field.append(jnp.concatenate([part[:points], part[points:]], axis=1))
        potential = dot(jnp.concatenate(field, axis=0), ri_ref[...])
        v_real = potential[:, :lanes] * weight
        v_imag = potential[:, lanes:] * weight
        p_real, p_imag = partner_parts(step)
        real = v_real * p_real - v_imag * p_imag
        imag = v_real * p_imag + v_imag * p_real
        total = jnp.where(low, real, imag) + pltpu.roll(jnp.where(low, imag, real), points, 1)
        o_v[step] = total.astype(bf16).reshape(quarter, points, lanes)
        put(step).start()
        return carry

    lax.fori_loop(0, 4, inverse, 0)
    for step in range(4):
        put(step).wait()


def exchange_part(place, occupations, slot_partner, pieces, first, second, coulomb, matrices):
    anywhere = pl.BlockSpec(memory_space=pl.ANY)
    scalar = pl.BlockSpec(memory_space=pltpu.SMEM)
    near = pl.BlockSpec(memory_space=pltpu.VMEM)
    planes = (4, quarter, points, lanes)
    return pl.pallas_call(
        pair_kernel,
        out_shape=jax.ShapeDtypeStruct(planes, bf16),
        in_specs=[scalar] * 3 + [anywhere] * 7 + [near] * 4,
        out_specs=anywhere,
        scratch_shapes=[
            pltpu.VMEM(planes, bf16),
            pltpu.VMEM(planes, bf16),
            pltpu.VMEM(planes, bf16),
            pltpu.VMEM((points, points, lanes), f32),
            pltpu.VMEM((2 * points * pitch, lanes), f32),
            pltpu.VMEM(planes, bf16),
            pltpu.SemaphoreType.DMA((4, 3)),
            pltpu.SemaphoreType.DMA,
            pltpu.SemaphoreType.DMA((4,)),
        ],
        compiler_params=pltpu.CompilerParams(vmem_limit_bytes=40 << 20),
        cost_estimate=pl.CostEstimate(
            flops=5 * 10**9, bytes_accessed=24 * 2**20, transcendentals=0
        ),
    )(place, occupations, slot_partner, *pieces, first, second, coulomb, *matrices)


def body(targets, partners, occupations, slot_partner, screening):
    own = targets[0]
    partner = partners[0]
    first = receive(partner, first_source)
    second = receive(partner, second_source)
    orders = [(0, 1), (1, 1), (1, 0), (0, 0)]
    halves = []
    for dy, dx in orders:
        same = own if (dy, dx) == (0, 0) else receive(own, offset_source(dy, dx, 0, 0))
        halves.append((same, receive(own, offset_source(dy, dx, 1, 0))))
    coulomb = coulomb_kernel(screening)
    matrices = section_matrices()
    device = lax.axis_index("tgt") * 4 + lax.axis_index("grp")
    slots = lax.dynamic_slice_in_dim(jnp.asarray(slot_table()), device, 1)[0]
    place = jnp.concatenate([lax.axis_index("grp")[None].astype(jnp.int32), slots])
    sibling = offset_source(0, 0, 0, 1)
    sums = []
    for n, ((dy, dx), (same, other)) in enumerate(zip(orders, halves)):
        pieces = [same, receive(same, sibling), other, receive(other, sibling)]
        if n >= 2:
            place, *sums[n - 2] = lax.optimization_barrier((place, *sums[n - 2]))
        part = exchange_part(
            place, occupations, slot_partner, pieces, first, second, coulomb, matrices
        )
        place, part = lax.optimization_barrier((place, part))
        both = []
        for dz in range(2):
            crossed = receive(part[2 * dz + 1], sibling)
            summed = part[2 * dz].astype(f32) + crossed.astype(f32)
            both.append(summed if (dy, dx, dz) == (0, 0, 0) else summed.astype(bf16))
        sums.append(both)
    terms = []
    for (dy, dx), both in zip(orders, sums):
        for dz in range(2):
            if (dy, dx, dz) == (0, 0, 0):
                terms.append(both[dz])
            else:
                arrived = receive(both[dz], offset_source(dy, dx, dz, 0))
                terms.append(arrived.astype(f32))
    return -sum(terms[1:], terms[0])[None]


def solution(mesh):
    in_specs = (P("tgt", "grp", None, None), P("tgt", None, None, None), P(), P(), P())
    out_specs = P("tgt", "grp", None, None)

    return jax.shard_map(body, mesh=mesh, in_specs=in_specs, out_specs=out_specs, check_vma=False)
```

```python
import functools
import math

import jax
import jax.numpy as jnp
import numpy as np
from jax import lax
from jax.experimental import pallas as pl
from jax.experimental.pallas import tpu as pltpu
from jax.sharding import PartitionSpec as P


coulomb_scale = 0.1
points = 64
lanes = 2 * points
quarter = 16
splits = 4
pitch = 72
axes = ("tgt", "grp")
f32 = jnp.float32
bf16 = jnp.bfloat16


devices = [
    (zh, y, x, zl, c)
    for zh in range(2)
    for y in range(4)
    for x in range(4)
    for zl in range(2)
    for c in range(2)
]
number = {device: i for i, device in enumerate(devices)}


def outer(i):
    return (i + 3) % 4 if i % 2 == 0 else (i + 1) % 4


def first_source(zh, y, x, zl, c):
    return {
        (0, 0): (zh, y, x, 0, 1),
        (0, 1): (zh ^ 1, y, x, 1, 0),
        (1, 0): (zh, outer(y), x, 1, 1),
        (1, 1): (zh ^ 1, y, outer(x), 0, 0),
    }[zl, c]


def second_source(zh, y, x, zl, c):
    return {
        (0, 0): (zh, outer(y), outer(x), 0, 1),
        (0, 1): (zh ^ 1, outer(y), outer(x), 1, 0),
        (1, 0): (zh, y, outer(x), 1, 1),
        (1, 1): (zh ^ 1, outer(y), x, 0, 0),
    }[zl, c]


def offset_source(dy, dx, dz, dc):
    return lambda zh, y, x, zl, c: (zh, y ^ dy, x ^ dx, zl ^ dz, c ^ dc)


def receive(value, source):
    pairs = [(number[source(*device)], number[device]) for device in devices]
    return lax.ppermute(value, axes, pairs)


def slot_table():
    slot = lambda d: (d[0] * 4 + d[1]) * 4 + d[2]
    return np.array(
        [[slot(first_source(*d)), slot(second_source(*d))] for d in devices], np.int32
    )


def tables():
    indices = np.arange(points)
    phases = indices[:, None] * indices[None, :] % points
    angles = phases.astype(np.float32) * np.float32(2.0 * math.pi / points)
    scale = np.float32(1.0 / math.sqrt(points))
    rounded = lambda t: (t * scale).astype(bf16).astype(np.float32)
    return rounded(np.cos(angles)), rounded(np.sin(angles))


def section_matrices():
    cosine, sine = tables()
    both = lambda t: np.kron(np.eye(2, dtype=np.float32), t)
    left_forward = np.block([[cosine, sine], [-sine, cosine]])
    left_inverse = np.block([[cosine, -sine], [sine, cosine]])
    right_forward = np.block([[both(cosine), both(-sine)], [both(sine), both(cosine)]])
    right_inverse = np.block([[both(cosine), both(sine)], [both(-sine), both(cosine)]])
    return [
        jnp.asarray(m, bf16) for m in (left_forward, left_inverse, right_forward, right_inverse)
    ]


def pair_weights(occupations, slot_partner, slots):
    ids = jnp.arange(occupations.shape[0], dtype=jnp.int32)
    match = slot_partner[:, None] == ids[None, :]
    by_slot = jnp.sum(jnp.where(match, occupations[None, :], 0.0), axis=1)
    return jnp.sum(jnp.where(slots[:, None] == ids[None, :], by_slot[None, :], 0.0), axis=1)


def coulomb_kernel(screening, weights):
    indices = jnp.arange(points, dtype=jnp.int32)
    signed = jnp.where(indices < points // 2, indices, indices - points).astype(f32) * (
        2.0 * math.pi / points
    )
    squares = signed * signed
    wave_sq = squares[:, None, None] + squares[None, :, None] + jnp.tile(squares, 2)[None, None, :]
    screen_wave = screening[0] * (2.0 * math.pi / points)
    lane = jnp.arange(lanes, dtype=jnp.int32)
    weight = jnp.where(lane < points, weights[0], weights[1])
    return (coulomb_scale / (wave_sq + screen_wave * screen_wave)) * weight[None, None, :]


def pair_kernel(
    place_ref, t0, t1, t2, t3, pa, pb, coulomb, lf_ref, li_ref, rf_ref, ri_ref,
    out,
    t_v, a_v, b_v, k_v, s_ref, z_ref, y_ref, o_v, in_sem, k_sem, out_sem,
):
    dot = functools.partial(jnp.dot, preferred_element_type=f32)
    place = place_ref[0]
    rows = quarter * points
    low = lax.broadcasted_iota(jnp.int16, (rows, lanes), 1) < points

    def block_of(step):
        return place ^ step

    def fetches(step, t_ref):
        planes = pl.ds(block_of(step) * quarter, quarter)
        return [
            pltpu.make_async_copy(t_ref, t_v.at[step], in_sem.at[step, 0]),
            pltpu.make_async_copy(pa.at[planes], a_v.at[step], in_sem.at[step, 1]),
            pltpu.make_async_copy(pb.at[planes], b_v.at[step], in_sem.at[step, 2]),
        ]

    for step, t_ref in enumerate((t0, t1, t2, t3)):
        for copy in fetches(step, t_ref):
            copy.start()
    k_copy = pltpu.make_async_copy(coulomb, k_v, k_sem)
    k_copy.start()
    lf = lf_ref[...]
    li = li_ref[...]

    def load(ref, step):
        return ref[step].reshape(rows, lanes)

    def swap(v):
        return pltpu.roll(v, points, 1)

    def last_section(field, matrix):
        part = rows // splits
        parts = [dot(field[n * part : (n + 1) * part], matrix).astype(bf16) for n in range(splits)]
        return jnp.concatenate(parts, axis=0)

    def arrive(step):
        for copy in fetches(step, t0):
            copy.wait()

    def forward_z(step):
        t = load(t_v, step)
        swapped = swap(t)
        t_real = jnp.where(low, t, swapped)
        t_imag = jnp.where(low, swapped, t)
        a = load(a_v, step)
        b = load(b_v, step)
        p_real = jnp.where(low, a, swap(b))
        p_imag = jnp.where(low, swap(a), b)
        a_v[step] = p_real.reshape(quarter, points, lanes)
        b_v[step] = p_imag.reshape(quarter, points, lanes)
        density = jnp.concatenate(
            [p_real * t_real + p_imag * t_imag, p_real * t_imag - p_imag * t_real], axis=1
        )
        along_z = last_section(density, rf_ref[...])
        slot = step % 2
        for j in range(quarter):
            for c in range(2):
                z_ref[slot, j, c * points : (c + 1) * points] = along_z[
                    j * points : (j + 1) * points, c * lanes : (c + 1) * lanes
                ]

    def forward_y(step):
        slot = step % 2
        plane = block_of(step) * quarter
        along_y = dot(lf, jnp.concatenate([z_ref[slot, j] for j in range(quarter)], axis=1))
        for j in range(quarter):
            s_ref[pl.ds(plane + j, lanes, stride=pitch), :] = along_y[:, j * lanes : (j + 1) * lanes]

    def forward(step, carry):
        arrive(step + 1)
        forward_y(step)
        forward_z(step + 1)
        return carry

    arrive(0)
    forward_z(0)
    lax.fori_loop(0, 3, forward, 0)
    forward_y(3)
    k_copy.wait()

    def line(k, part):
        return pl.ds(pl.multiple_of((part * points + k) * pitch, 8), points)

    def middle(i, carry):
        first = i * quarter
        columns = []
        for j in range(quarter):
            parts = [s_ref[line(first + j, part), :].astype(bf16) for part in range(2)]
            columns.append(jnp.concatenate(parts, axis=0))
        spectrum = dot(lf, jnp.concatenate(columns, axis=1))
        weights = jnp.concatenate([k_v[first + j] for j in range(quarter)], axis=1)
        scaled = (spectrum * jnp.concatenate([weights, weights], axis=0)).astype(bf16)
        along_x = dot(li, scaled)
        for j in range(quarter):
            for part in range(2):
                s_ref[line(first + j, part), :] = along_x[
                    part * points : (part + 1) * points, j * lanes : (j + 1) * lanes
                ]
        return carry

    lax.fori_loop(0, 4, middle, 0)

    def put(step):
        return pltpu.make_async_copy(o_v.at[step], out.at[step], out_sem.at[step])

    def inverse_y(step):
        slot = step % 2
        plane = block_of(step) * quarter
        columns = [
            s_ref[pl.ds(plane + j, lanes, stride=pitch), :].astype(bf16) for j in range(quarter)
        ]
        along_y = dot(li, jnp.concatenate(columns, axis=1)).astype(bf16)
        for j in range(quarter):
            for c in range(2):
                y_ref[slot, j * points : (j + 1) * points, c * lanes : (c + 1) * lanes] = along_y[
                    c * points : (c + 1) * points, j * lanes : (j + 1) * lanes
                ]

    def inverse_z(step):
        potential = last_section(y_ref[step % 2], ri_ref[...])
        v_real = potential[:, :lanes]
        v_imag = potential[:, lanes:]
        p_real = load(a_v, step)
        p_imag = load(b_v, step)
        real = v_real * p_real - v_imag * p_imag
        imag = v_real * p_imag + v_imag * p_real
        total = jnp.where(low, real, imag) + swap(jnp.where(low, imag, real))
        o_v[step] = total.reshape(quarter, points, lanes)

    def inverse(step, carry):
        inverse_z(step)
        inverse_y(step + 1)
        put(step).start()
        return carry

    inverse_y(0)
    lax.fori_loop(0, 3, inverse, 0)
    inverse_z(3)
    put(3).start()
    for step in range(4):
        put(step).wait()


def exchange_part(place, pieces, first, second, coulomb, matrices):
    anywhere = pl.BlockSpec(memory_space=pl.ANY)
    scalar = pl.BlockSpec(memory_space=pltpu.SMEM)
    near = pl.BlockSpec(memory_space=pltpu.VMEM)
    planes = (4, quarter, points, lanes)
    return pl.pallas_call(
        pair_kernel,
        out_shape=jax.ShapeDtypeStruct(planes, bf16),
        in_specs=[scalar] + [anywhere] * 7 + [near] * 4,
        out_specs=anywhere,
        scratch_shapes=[
            pltpu.VMEM(planes, bf16),
            pltpu.VMEM(planes, bf16),
            pltpu.VMEM(planes, bf16),
            pltpu.VMEM((points, points, lanes), f32),
            pltpu.VMEM((2 * points * pitch, lanes), f32),
            pltpu.VMEM((2, quarter, lanes, lanes), bf16),
            pltpu.VMEM((2, quarter * points, 2 * lanes), bf16),
            pltpu.VMEM(planes, bf16),
            pltpu.SemaphoreType.DMA((4, 3)),
            pltpu.SemaphoreType.DMA,
            pltpu.SemaphoreType.DMA((4,)),
        ],
        compiler_params=pltpu.CompilerParams(vmem_limit_bytes=40 << 20),
        cost_estimate=pl.CostEstimate(
            flops=5 * 10**9, bytes_accessed=24 * 2**20, transcendentals=0
        ),
    )(place, *pieces, first, second, coulomb, *matrices)


def body(targets, partners, occupations, slot_partner, screening):
    own = targets[0]
    partner = partners[0]
    first = receive(partner, first_source)
    second = receive(partner, second_source)
    orders = [(0, 1), (1, 0), (1, 1), (0, 0)]
    halves = []
    for dy, dx in orders:
        same = own if (dy, dx) == (0, 0) else receive(own, offset_source(dy, dx, 0, 0))
        halves.append((same, receive(own, offset_source(dy, dx, 1, 0))))
    matrices = section_matrices()
    device = lax.axis_index("tgt") * 4 + lax.axis_index("grp")
    slots = lax.dynamic_slice_in_dim(jnp.asarray(slot_table()), device, 1)[0]
    place = lax.axis_index("grp")[None].astype(jnp.int32)
    coulomb = coulomb_kernel(screening, pair_weights(occupations, slot_partner, slots))
    sibling = offset_source(0, 0, 0, 1)
    sums = []
    marks = []
    for n, ((dy, dx), (same, other)) in enumerate(zip(orders, halves)):
        if n >= 2:
            _, same, other = lax.optimization_barrier((marks[n - 2], same, other))
        pieces = [same, receive(same, sibling), other, receive(other, sibling)]
        for m in {2: [0], 3: [1, 2]}.get(n, []):
            place, *sums[m] = lax.optimization_barrier((place, *sums[m]))
        part = exchange_part(place, pieces, first, second, coulomb, matrices)
        place, part = lax.optimization_barrier((place, part))
        marks.append(place)
        both = []
        for dz in range(2):
            crossed = receive(part[2 * dz + 1], sibling)
            summed = part[2 * dz].astype(f32) + crossed.astype(f32)
            both.append(summed if (dy, dx, dz) == (0, 0, 0) else summed.astype(bf16))
        sums.append(both)
    terms = []
    for (dy, dx), both in zip(orders, sums):
        for dz in range(2):
            if (dy, dx, dz) == (0, 0, 0):
                terms.append(both[dz])
            else:
                arrived = receive(both[dz], offset_source(dy, dx, dz, 0))
                terms.append(arrived.astype(f32))
    return -sum(terms[1:], terms[0])[None]


def solution(mesh):
    in_specs = (P("tgt", "grp", None, None), P("tgt", None, None, None), P(), P(), P())
    out_specs = P("tgt", "grp", None, None)

    return jax.shard_map(body, mesh=mesh, in_specs=in_specs, out_specs=out_specs, check_vma=False)
```

```python
import functools
import math

import jax
import jax.numpy as jnp
import numpy as np
from jax import lax
from jax.experimental import pallas as pl
from jax.experimental.pallas import tpu as pltpu
from jax.sharding import PartitionSpec as P


coulomb_scale = 0.1
points = 64
lanes = 2 * points
quarter = 16
splits = 4
pitch = 72
axes = ("tgt", "grp")
f32 = jnp.float32
bf16 = jnp.bfloat16


devices = [
    (zh, y, x, zl, c)
    for zh in range(2)
    for y in range(4)
    for x in range(4)
    for zl in range(2)
    for c in range(2)
]
number = {device: i for i, device in enumerate(devices)}


def outer(i):
    return (i + 3) % 4 if i % 2 == 0 else (i + 1) % 4


def first_source(zh, y, x, zl, c):
    return {
        (0, 0): (zh, y, x, 0, 1),
        (0, 1): (zh ^ 1, y, x, 1, 0),
        (1, 0): (zh, outer(y), x, 1, 1),
        (1, 1): (zh ^ 1, y, outer(x), 0, 0),
    }[zl, c]


def second_source(zh, y, x, zl, c):
    return {
        (0, 0): (zh, outer(y), outer(x), 0, 1),
        (0, 1): (zh ^ 1, outer(y), outer(x), 1, 0),
        (1, 0): (zh, y, outer(x), 1, 1),
        (1, 1): (zh ^ 1, outer(y), x, 0, 0),
    }[zl, c]


def offset_source(dy, dx, dz, dc):
    return lambda zh, y, x, zl, c: (zh, y ^ dy, x ^ dx, zl ^ dz, c ^ dc)


def receive(value, source):
    pairs = [(number[source(*device)], number[device]) for device in devices]
    return lax.ppermute(value, axes, pairs)


def slot_table():
    slot = lambda d: (d[0] * 4 + d[1]) * 4 + d[2]
    return np.array(
        [[slot(first_source(*d)), slot(second_source(*d))] for d in devices], np.int32
    )


def tables():
    indices = np.arange(points)
    phases = indices[:, None] * indices[None, :] % points
    angles = phases.astype(np.float32) * np.float32(2.0 * math.pi / points)
    scale = np.float32(1.0 / math.sqrt(points))
    rounded = lambda t: (t * scale).astype(bf16).astype(np.float32)
    return rounded(np.cos(angles)), rounded(np.sin(angles))


def section_matrices():
    cosine, sine = tables()
    both = lambda t: np.kron(np.eye(2, dtype=np.float32), t)
    left_forward = np.block([[cosine, sine], [-sine, cosine]])
    left_inverse = np.block([[cosine, -sine], [sine, cosine]])
    right_forward = np.block([[both(cosine), both(-sine)], [both(sine), both(cosine)]])
    right_inverse = np.block([[both(cosine), both(sine)], [both(-sine), both(cosine)]])
    return [
        jnp.asarray(m, bf16) for m in (left_forward, left_inverse, right_forward, right_inverse)
    ]


def pair_weights(occupations, slot_partner, slots):
    ids = jnp.arange(occupations.shape[0], dtype=jnp.int32)
    match = slot_partner[:, None] == ids[None, :]
    by_slot = jnp.sum(jnp.where(match, occupations[None, :], 0.0), axis=1)
    return jnp.sum(jnp.where(slots[:, None] == ids[None, :], by_slot[None, :], 0.0), axis=1)


def coulomb_kernel(screening, weights):
    indices = jnp.arange(points, dtype=jnp.int32)
    signed = jnp.where(indices < points // 2, indices, indices - points).astype(f32) * (
        2.0 * math.pi / points
    )
    squares = signed * signed
    wave_sq = squares[:, None, None] + squares[None, :, None] + jnp.tile(squares, 2)[None, None, :]
    screen_wave = screening[0] * (2.0 * math.pi / points)
    lane = jnp.arange(lanes, dtype=jnp.int32)
    weight = jnp.where(lane < points, weights[0], weights[1])
    return (coulomb_scale / (wave_sq + screen_wave * screen_wave)) * weight[None, None, :]


def pair_kernel(two_targets, stage, *refs):
    refs = list(refs)
    take = lambda count: [refs.pop(0) for _ in range(count)]
    (place_ref,) = take(1)
    if two_targets:
        targets = [take(4), take(4)]
        (shared,) = take(1)
    else:
        shared = take(4)
        partners = take(2)
    coulomb, lf_ref, li_ref, rf_ref, ri_ref = take(5)
    earlier = take(2) if stage == "last" else []
    outs = take(2 if two_targets else 1)
    x_v, a_v, b_v, k_v, s_ref, z_ref, y_ref, o_v, e_v, in_sem, k_sem, e_sem, out_sem = refs

    dot = functools.partial(jnp.dot, preferred_element_type=f32)
    place = place_ref[0]
    rows = quarter * points
    low = lax.broadcasted_iota(jnp.int16, (rows, lanes), 1) < points

    def block_of(step):
        return place ^ step

    def fetches(step, n):
        planes = pl.ds(block_of(step) * quarter, quarter)
        if two_targets:
            sources = [shared.at[planes], targets[0][n], targets[1][n]]
        else:
            sources = [shared[n], partners[0].at[planes], partners[1].at[planes]]
        return [
            pltpu.make_async_copy(source, v.at[step], in_sem.at[step, i])
            for i, (source, v) in enumerate(zip(sources, (x_v, a_v, b_v)))
        ]

    for step in range(4):
        for copy in fetches(step, step):
            copy.start()
    k_copy = pltpu.make_async_copy(coulomb, k_v, k_sem)
    k_copy.start()
    e_copies = [
        pltpu.make_async_copy(source, e_v.at[i], e_sem.at[i]) for i, source in enumerate(earlier)
    ]
    for copy in e_copies:
        copy.start()
    lf = lf_ref[...]
    li = li_ref[...]

    def load(ref, step):
        return ref[step].reshape(rows, lanes)

    def swap(v):
        return pltpu.roll(v, points, 1)

    def planes_of(v):
        return v.reshape(quarter, points, lanes)

    def last_section(field, matrix):
        part = rows // splits
        parts = [dot(field[n * part : (n + 1) * part], matrix).astype(bf16) for n in range(splits)]
        return jnp.concatenate(parts, axis=0)

    def arrive(step):
        for copy in fetches(step, 0):
            copy.wait()

    def forward_z(step):
        x = load(x_v, step)
        swapped = swap(x)
        x_real = jnp.where(low, x, swapped)
        x_imag = jnp.where(low, swapped, x)
        a = load(a_v, step)
        b = load(b_v, step)
        q_real = jnp.where(low, a, swap(b))
        q_imag = jnp.where(low, swap(a), b)
        p_real, p_imag = (x_real, x_imag) if two_targets else (q_real, q_imag)
        t_real, t_imag = (q_real, q_imag) if two_targets else (x_real, x_imag)
        a_v[step] = planes_of(p_real)
        b_v[step] = planes_of(p_imag)
        density = jnp.concatenate(
            [p_real * t_real + p_imag * t_imag, p_real * t_imag - p_imag * t_real], axis=1
        )
        along_z = last_section(density, rf_ref[...])
        slot = step % 2
        for j in range(quarter):
            for c in range(2):
                z_ref[slot, j, c * points : (c + 1) * points] = along_z[
                    j * points : (j + 1) * points, c * lanes : (c + 1) * lanes
                ]

    def forward_y(step):
        slot = step % 2
        plane = block_of(step) * quarter
        along_y = dot(lf, jnp.concatenate([z_ref[slot, j] for j in range(quarter)], axis=1))
        for j in range(quarter):
            s_ref[pl.ds(plane + j, lanes, stride=pitch), :] = along_y[:, j * lanes : (j + 1) * lanes]

    def forward(step, carry):
        arrive(step + 1)
        forward_y(step)
        forward_z(step + 1)
        return carry

    arrive(0)
    forward_z(0)
    lax.fori_loop(0, 3, forward, 0)
    forward_y(3)
    k_copy.wait()

    def line(k, part):
        return pl.ds(pl.multiple_of((part * points + k) * pitch, 8), points)

    def middle(i, carry):
        first = i * quarter
        columns = []
        for j in range(quarter):
            parts = [s_ref[line(first + j, part), :].astype(bf16) for part in range(2)]
            columns.append(jnp.concatenate(parts, axis=0))
        spectrum = dot(lf, jnp.concatenate(columns, axis=1))
        weights = jnp.concatenate([k_v[first + j] for j in range(quarter)], axis=1)
        scaled = (spectrum * jnp.concatenate([weights, weights], axis=0)).astype(bf16)
        along_x = dot(li, scaled)
        for j in range(quarter):
            for part in range(2):
                s_ref[line(first + j, part), :] = along_x[
                    part * points : (part + 1) * points, j * lanes : (j + 1) * lanes
                ]
        return carry

    lax.fori_loop(0, 4, middle, 0)
    for copy in e_copies:
        copy.wait()

    def put(step):
        return [
            pltpu.make_async_copy(o_v.at[i, step], out.at[step], out_sem.at[i, step])
            for i, out in enumerate(outs)
        ]

    def inverse_y(step):
        slot = step % 2
        plane = block_of(step) * quarter
        columns = [
            s_ref[pl.ds(plane + j, lanes, stride=pitch), :].astype(bf16) for j in range(quarter)
        ]
        along_y = dot(li, jnp.concatenate(columns, axis=1)).astype(bf16)
        for j in range(quarter):
            for c in range(2):
                y_ref[slot, j * points : (j + 1) * points, c * lanes : (c + 1) * lanes] = along_y[
                    c * points : (c + 1) * points, j * lanes : (j + 1) * lanes
                ]

    def inverse_z(step):
        potential = last_section(y_ref[step % 2], ri_ref[...])
        v_real = potential[:, :lanes]
        v_imag = potential[:, lanes:]
        p_real = load(a_v, step)
        p_imag = load(b_v, step)
        real = v_real * p_real - v_imag * p_imag
        imag = v_real * p_imag + v_imag * p_real
        if stage == "first":
            results = [real, imag]
        elif stage == "last":
            real = real + e_v[0, step].reshape(rows, lanes)
            imag = imag + e_v[1, step].reshape(rows, lanes)
            results = [jnp.where(low, real, swap(imag)), jnp.where(low, swap(real), imag)]
        else:
            results = [jnp.where(low, real, imag) + swap(jnp.where(low, imag, real))]
        for i, result in enumerate(results):
            o_v[i, step] = planes_of(result)

    def inverse(step, carry):
        inverse_z(step)
        inverse_y(step + 1)
        for copy in put(step):
            copy.start()
        return carry

    inverse_y(0)
    lax.fori_loop(0, 3, inverse, 0)
    inverse_z(3)
    for copy in put(3):
        copy.start()
    for step in range(4):
        for copy in put(step):
            copy.wait()


def exchange_part(place, sides, coulomb, matrices, two_targets=False, stage="only", earlier=()):
    anywhere = pl.BlockSpec(memory_space=pl.ANY)
    scalar = pl.BlockSpec(memory_space=pltpu.SMEM)
    near = pl.BlockSpec(memory_space=pltpu.VMEM)
    planes = (4, quarter, points, lanes)
    both = (2, *planes)
    outs = 2 if two_targets else 1
    return pl.pallas_call(
        functools.partial(pair_kernel, two_targets, stage),
        out_shape=[jax.ShapeDtypeStruct(planes, bf16)] * outs,
        in_specs=[scalar]
        + [anywhere] * (len(sides) + 1)
        + [near] * 4
        + [anywhere] * len(earlier),
        out_specs=[anywhere] * outs,
        scratch_shapes=[
            pltpu.VMEM(planes, bf16),
            pltpu.VMEM(planes, bf16),
            pltpu.VMEM(planes, bf16),
            pltpu.VMEM((points, points, lanes), f32),
            pltpu.VMEM((2 * points * pitch, lanes), f32),
            pltpu.VMEM((2, quarter, lanes, lanes), bf16),
            pltpu.VMEM((2, quarter * points, 2 * lanes), bf16),
            pltpu.VMEM(both, bf16),
            pltpu.VMEM(both, bf16),
            pltpu.SemaphoreType.DMA((4, 3)),
            pltpu.SemaphoreType.DMA,
            pltpu.SemaphoreType.DMA((2,)),
            pltpu.SemaphoreType.DMA((2, 4)),
        ],
        compiler_params=pltpu.CompilerParams(vmem_limit_bytes=40 << 20),
        cost_estimate=pl.CostEstimate(
            flops=5 * 10**9, bytes_accessed=24 * 2**20, transcendentals=0
        ),
    )(place, *sides, coulomb, *matrices, *earlier)


def body(targets, partners, occupations, slot_partner, screening):
    own = targets[0]
    partner = partners[0]
    first = receive(partner, first_source)
    orders = [(0, 1), (1, 0), (1, 1), (0, 0)]
    halves = []
    for dy, dx in orders:
        half = []
        for dz in range(2):
            source = offset_source(dy, dx, dz, 0)
            half.append(own if (dy, dx, dz) == (0, 0, 0) else receive(own, source))
        halves.append(half)
    second = receive(partner, second_source)
    matrices = section_matrices()
    device = lax.axis_index("tgt") * 4 + lax.axis_index("grp")
    slots = lax.dynamic_slice_in_dim(jnp.asarray(slot_table()), device, 1)[0]
    place = lax.axis_index("grp")[None].astype(jnp.int32)
    weights = pair_weights(occupations, slot_partner, slots)
    sibling = offset_source(0, 0, 0, 1)

    def pieces(n, mark=None):
        same, other = halves[n]
        if mark is not None:
            _, same, other = lax.optimization_barrier((mark, same, other))
        return [same, receive(same, sibling), other, receive(other, sibling)]

    def core_sum(part, rounded):
        both = []
        for dz in range(2):
            crossed = receive(part[2 * dz + 1], sibling)
            summed = part[2 * dz].astype(f32) + crossed.astype(f32)
            both.append(summed.astype(bf16) if rounded[dz] else summed)
        return both

    def call(place, *args, **kwargs):
        parts = exchange_part(place, *args, **kwargs)
        return lax.optimization_barrier((place, *parts))

    two = pieces(0) + pieces(1)
    coulombs = [
        coulomb_kernel(screening, (weights[a], weights[b])) for a, b in ((0, 0), (1, 1), (0, 1))
    ]
    place, *earlier = call(
        place, two + [first], coulombs[0], matrices, two_targets=True, stage="first"
    )
    mark = place
    place, *parts = call(place, two + [second], coulombs[1], matrices, True, "last", earlier)
    sums = [core_sum(part, (True, True)) for part in parts]
    place, *flat = lax.optimization_barrier((place, *sums[0], *sums[1]))
    sums = [flat[:2], flat[2:]]
    place, part = call(place, pieces(2, mark) + [first, second], coulombs[2], matrices)
    sums.append(core_sum(part, (True, True)))
    place, *sums[2] = lax.optimization_barrier((place, *sums[2]))
    place, part = call(place, pieces(3, mark) + [first, second], coulombs[2], matrices)
    sums.append(core_sum(part, (False, True)))
    terms = []
    for (dy, dx), both in zip(orders, sums):
        for dz in range(2):
            if (dy, dx, dz) == (0, 0, 0):
                terms.append(both[dz])
            else:
                arrived = receive(both[dz], offset_source(dy, dx, dz, 0))
                terms.append(arrived.astype(f32))
    return -sum(terms[1:], terms[0])[None]


def solution(mesh):
    in_specs = (P("tgt", "grp", None, None), P("tgt", None, None, None), P(), P(), P())
    out_specs = P("tgt", "grp", None, None)

    return jax.shard_map(body, mesh=mesh, in_specs=in_specs, out_specs=out_specs, check_vma=False)
```

```python
import functools
import math

import jax
import jax.numpy as jnp
import numpy as np
from jax import lax
from jax.experimental import pallas as pl
from jax.experimental.pallas import tpu as pltpu
from jax.sharding import PartitionSpec as P


coulomb_scale = 0.1
points = 64
lanes = 2 * points
quarter = 16
splits = 4
pitch = 72
axes = ("tgt", "grp")
f32 = jnp.float32
bf16 = jnp.bfloat16


devices = [
    (zh, y, x, zl, c)
    for zh in range(2)
    for y in range(4)
    for x in range(4)
    for zl in range(2)
    for c in range(2)
]
number = {device: i for i, device in enumerate(devices)}


def outer(i):
    return (i + 3) % 4 if i % 2 == 0 else (i + 1) % 4


def first_source(zh, y, x, zl, c):
    return {
        (0, 0): (zh, y, x, 0, 1),
        (0, 1): (zh ^ 1, y, x, 1, 0),
        (1, 0): (zh, outer(y), x, 1, 1),
        (1, 1): (zh ^ 1, y, outer(x), 0, 0),
    }[zl, c]


def second_source(zh, y, x, zl, c):
    return {
        (0, 0): (zh, outer(y), outer(x), 0, 1),
        (0, 1): (zh ^ 1, outer(y), outer(x), 1, 0),
        (1, 0): (zh, y, outer(x), 1, 1),
        (1, 1): (zh ^ 1, outer(y), x, 0, 0),
    }[zl, c]


def offset_source(dy, dx, dz, dc):
    return lambda zh, y, x, zl, c: (zh, y ^ dy, x ^ dx, zl ^ dz, c ^ dc)


def receive(value, source):
    pairs = [(number[source(*device)], number[device]) for device in devices]
    return lax.ppermute(value, axes, pairs)


def slot_table():
    slot = lambda d: (d[0] * 4 + d[1]) * 4 + d[2]
    return np.array(
        [[slot(first_source(*d)), slot(second_source(*d))] for d in devices], np.int32
    )


def tables():
    indices = np.arange(points)
    phases = indices[:, None] * indices[None, :] % points
    angles = phases.astype(np.float32) * np.float32(2.0 * math.pi / points)
    scale = np.float32(1.0 / math.sqrt(points))
    rounded = lambda t: (t * scale).astype(bf16).astype(np.float32)
    return rounded(np.cos(angles)), rounded(np.sin(angles))


def section_matrices():
    cosine, sine = tables()
    both = lambda t: np.kron(np.eye(2, dtype=np.float32), t)
    left_forward = np.block([[cosine, sine], [-sine, cosine]])
    left_inverse = np.block([[cosine, -sine], [sine, cosine]])
    right_forward = np.block([[both(cosine), both(-sine)], [both(sine), both(cosine)]])
    right_inverse = np.block([[both(cosine), both(sine)], [both(-sine), both(cosine)]])
    return [
        jnp.asarray(m, bf16) for m in (left_forward, left_inverse, right_forward, right_inverse)
    ]


def pair_weights(occupations, slot_partner, slots):
    ids = jnp.arange(occupations.shape[0], dtype=jnp.int32)
    match = slot_partner[:, None] == ids[None, :]
    by_slot = jnp.sum(jnp.where(match, occupations[None, :], 0.0), axis=1)
    return jnp.sum(jnp.where(slots[:, None] == ids[None, :], by_slot[None, :], 0.0), axis=1)


def coulomb_kernel(screening, weights):
    indices = jnp.arange(points, dtype=jnp.int32)
    signed = jnp.where(indices < points // 2, indices, indices - points).astype(f32) * (
        2.0 * math.pi / points
    )
    squares = signed * signed
    wave_sq = squares[:, None, None] + squares[None, :, None] + jnp.tile(squares, 2)[None, None, :]
    screen_wave = screening[0] * (2.0 * math.pi / points)
    lane = jnp.arange(lanes, dtype=jnp.int32)
    weight = jnp.where(lane < points, weights[0], weights[1])
    return (coulomb_scale / (wave_sq + screen_wave * screen_wave)) * weight[None, None, :]


def pair_kernel(two_targets, stage, *refs):
    refs = list(refs)
    take = lambda count: [refs.pop(0) for _ in range(count)]
    (place_ref,) = take(1)
    if two_targets:
        targets = [take(4), take(4)]
        (shared,) = take(1)
    else:
        shared = take(4)
        partners = take(2)
    coulomb, lf_ref, li_ref, rf_ref, ri_ref = take(5)
    earlier = take(2) if stage == "last" else []
    outs = take(2 if two_targets else 1)
    x_v, a_v, b_v, k_v, s_ref, z_ref, y_ref, o_v, e_v, in_sem, k_sem, e_sem, out_sem = refs

    dot = functools.partial(jnp.dot, preferred_element_type=f32)
    place = place_ref[0]
    rows = quarter * points
    low = lax.broadcasted_iota(jnp.int16, (rows, lanes), 1) < points

    def block_of(step):
        return place ^ step

    def fetches(step, n):
        planes = pl.ds(block_of(step) * quarter, quarter)
        if two_targets:
            sources = [shared.at[planes], targets[0][n], targets[1][n]]
        else:
            sources = [shared[n], partners[0].at[planes], partners[1].at[planes]]
        return [
            pltpu.make_async_copy(source, v.at[step], in_sem.at[step, i])
            for i, (source, v) in enumerate(zip(sources, (x_v, a_v, b_v)))
        ]

    for step in range(4):
        for copy in fetches(step, step):
            copy.start()
    k_copy = pltpu.make_async_copy(coulomb, k_v, k_sem)
    k_copy.start()
    e_copies = [
        pltpu.make_async_copy(source, e_v.at[i], e_sem.at[i]) for i, source in enumerate(earlier)
    ]
    for copy in e_copies:
        copy.start()
    lf = lf_ref[...]
    li = li_ref[...]

    def load(ref, step):
        return ref[step].reshape(rows, lanes)

    def swap(v):
        return pltpu.roll(v, points, 1)

    def planes_of(v):
        return v.reshape(quarter, points, lanes)

    def last_section(field, matrix):
        part = rows // splits
        parts = [dot(field[n * part : (n + 1) * part], matrix).astype(bf16) for n in range(splits)]
        return jnp.concatenate(parts, axis=0)

    def arrive(step):
        for copy in fetches(step, 0):
            copy.wait()

    def forward_z(step):
        x = load(x_v, step)
        swapped = swap(x)
        x_real = jnp.where(low, x, swapped)
        x_imag = jnp.where(low, swapped, x)
        a = load(a_v, step)
        b = load(b_v, step)
        q_real = jnp.where(low, a, swap(b))
        q_imag = jnp.where(low, swap(a), b)
        p_real, p_imag = (x_real, x_imag) if two_targets else (q_real, q_imag)
        t_real, t_imag = (q_real, q_imag) if two_targets else (x_real, x_imag)
        a_v[step] = planes_of(p_real)
        b_v[step] = planes_of(p_imag)
        density = jnp.concatenate(
            [p_real * t_real + p_imag * t_imag, p_real * t_imag - p_imag * t_real], axis=1
        )
        along_z = last_section(density, rf_ref[...])
        slot = step % 2
        for j in range(quarter):
            for c in range(2):
                z_ref[slot, j, c * points : (c + 1) * points] = along_z[
                    j * points : (j + 1) * points, c * lanes : (c + 1) * lanes
                ]

    def forward_y(step):
        slot = step % 2
        plane = block_of(step) * quarter
        along_y = dot(lf, jnp.concatenate([z_ref[slot, j] for j in range(quarter)], axis=1))
        for j in range(quarter):
            s_ref[pl.ds(plane + j, lanes, stride=pitch), :] = along_y[:, j * lanes : (j + 1) * lanes]

    def forward(step, carry):
        arrive(step + 1)
        forward_y(step)
        forward_z(step + 1)
        return carry

    arrive(0)
    forward_z(0)
    lax.fori_loop(0, 3, forward, 0)
    forward_y(3)
    k_copy.wait()

    def line(k, part):
        return pl.ds(pl.multiple_of((part * points + k) * pitch, 8), points)

    def middle(i, carry):
        first = i * quarter
        columns = []
        for j in range(quarter):
            parts = [s_ref[line(first + j, part), :].astype(bf16) for part in range(2)]
            columns.append(jnp.concatenate(parts, axis=0))
        spectrum = dot(lf, jnp.concatenate(columns, axis=1))
        weights = jnp.concatenate([k_v[first + j] for j in range(quarter)], axis=1)
        scaled = (spectrum * jnp.concatenate([weights, weights], axis=0)).astype(bf16)
        along_x = dot(li, scaled)
        for j in range(quarter):
            for part in range(2):
                s_ref[line(first + j, part), :] = along_x[
                    part * points : (part + 1) * points, j * lanes : (j + 1) * lanes
                ]
        return carry

    lax.fori_loop(0, 4, middle, 0)
    for copy in e_copies:
        copy.wait()

    def put(step):
        return [
            pltpu.make_async_copy(o_v.at[i, step], out.at[step], out_sem.at[i, step])
            for i, out in enumerate(outs)
        ]

    def inverse_y(step):
        slot = step % 2
        plane = block_of(step) * quarter
        columns = [
            s_ref[pl.ds(plane + j, lanes, stride=pitch), :].astype(bf16) for j in range(quarter)
        ]
        along_y = dot(li, jnp.concatenate(columns, axis=1)).astype(bf16)
        for j in range(quarter):
            for c in range(2):
                y_ref[slot, j * points : (j + 1) * points, c * lanes : (c + 1) * lanes] = along_y[
                    c * points : (c + 1) * points, j * lanes : (j + 1) * lanes
                ]

    def inverse_z(step):
        potential = last_section(y_ref[step % 2], ri_ref[...])
        v_real = potential[:, :lanes]
        v_imag = potential[:, lanes:]
        p_real = load(a_v, step)
        p_imag = load(b_v, step)
        real = v_real * p_real - v_imag * p_imag
        imag = v_real * p_imag + v_imag * p_real
        if stage == "first":
            results = [real, imag]
        elif stage == "last":
            real = real + e_v[0, step].reshape(rows, lanes)
            imag = imag + e_v[1, step].reshape(rows, lanes)
            results = [jnp.where(low, real, swap(imag)), jnp.where(low, swap(real), imag)]
        else:
            results = [jnp.where(low, real, imag) + swap(jnp.where(low, imag, real))]
        for i, result in enumerate(results):
            o_v[i, step] = planes_of(result)

    def inverse(step, carry):
        inverse_z(step)
        inverse_y(step + 1)
        for copy in put(step):
            copy.start()
        return carry

    inverse_y(0)
    lax.fori_loop(0, 3, inverse, 0)
    inverse_z(3)
    for copy in put(3):
        copy.start()
    for step in range(4):
        for copy in put(step):
            copy.wait()


def exchange_part(place, sides, coulomb, matrices, two_targets=False, stage="only", earlier=()):
    anywhere = pl.BlockSpec(memory_space=pl.ANY)
    scalar = pl.BlockSpec(memory_space=pltpu.SMEM)
    near = pl.BlockSpec(memory_space=pltpu.VMEM)
    planes = (4, quarter, points, lanes)
    both = (2, *planes)
    outs = 2 if two_targets else 1
    return pl.pallas_call(
        functools.partial(pair_kernel, two_targets, stage),
        out_shape=[jax.ShapeDtypeStruct(planes, bf16)] * outs,
        in_specs=[scalar]
        + [anywhere] * (len(sides) + 1)
        + [near] * 4
        + [anywhere] * len(earlier),
        out_specs=[anywhere] * outs,
        scratch_shapes=[
            pltpu.VMEM(planes, bf16),
            pltpu.VMEM(planes, bf16),
            pltpu.VMEM(planes, bf16),
            pltpu.VMEM((points, points, lanes), f32),
            pltpu.VMEM((2 * points * pitch, lanes), f32),
            pltpu.VMEM((2, quarter, lanes, lanes), bf16),
            pltpu.VMEM((2, quarter * points, 2 * lanes), bf16),
            pltpu.VMEM(both, bf16),
            pltpu.VMEM(both, bf16),
            pltpu.SemaphoreType.DMA((4, 3)),
            pltpu.SemaphoreType.DMA,
            pltpu.SemaphoreType.DMA((2,)),
            pltpu.SemaphoreType.DMA((2, 4)),
        ],
        compiler_params=pltpu.CompilerParams(vmem_limit_bytes=40 << 20),
        cost_estimate=pl.CostEstimate(
            flops=5 * 10**9, bytes_accessed=24 * 2**20, transcendentals=0
        ),
    )(place, *sides, coulomb, *matrices, *earlier)


def body(targets, partners, occupations, slot_partner, screening):
    own = targets[0]
    partner = partners[0]
    first = receive(partner, first_source)
    orders = [(0, 1), (1, 0), (1, 1), (0, 0)]
    halves = []
    sent = own
    for n, (dy, dx) in enumerate(orders):
        if n == 2:
            sent, *halves[1] = lax.optimization_barrier((own, *halves[1]))
        half = []
        for dz in range(2):
            source = offset_source(dy, dx, dz, 0)
            half.append(own if (dy, dx, dz) == (0, 0, 0) else receive(sent, source))
        halves.append(half)
    second = receive(partner, second_source)
    matrices = section_matrices()
    device = lax.axis_index("tgt") * 4 + lax.axis_index("grp")
    slots = lax.dynamic_slice_in_dim(jnp.asarray(slot_table()), device, 1)[0]
    place = lax.axis_index("grp")[None].astype(jnp.int32)
    weights = pair_weights(occupations, slot_partner, slots)
    sibling = offset_source(0, 0, 0, 1)

    def pieces(n, mark=None):
        same, other = halves[n]
        if mark is not None:
            _, same, other = lax.optimization_barrier((mark, same, other))
        crossed = []
        for piece in (same, other):
            crossed.append(receive(piece, sibling))
        return [same, crossed[0], other, crossed[1]]

    def core_sum(part, rounded):
        both = []
        for dz in range(2):
            crossed = receive(part[2 * dz + 1], sibling)
            summed = part[2 * dz].astype(f32) + crossed.astype(f32)
            both.append(summed.astype(bf16) if rounded[dz] else summed)
        return both

    def call(place, *args, **kwargs):
        parts = exchange_part(place, *args, **kwargs)
        return lax.optimization_barrier((place, *parts))

    coulombs = [
        coulomb_kernel(screening, (weights[a], weights[b])) for a, b in ((0, 0), (1, 1), (0, 1))
    ]
    *coulombs, halves[0][1], halves[1][1] = lax.optimization_barrier(
        (*coulombs, halves[0][1], halves[1][1])
    )
    two = pieces(0) + pieces(1)
    place, *earlier = call(
        place, two + [first], coulombs[0], matrices, two_targets=True, stage="first"
    )
    mark = place
    place, *parts = call(place, two + [second], coulombs[1], matrices, True, "last", earlier)
    sums = [core_sum(part, (True, True)) for part in parts]
    place, *flat = lax.optimization_barrier((place, *sums[0], *sums[1]))
    sums = [flat[:2], flat[2:]]
    place, part = call(place, pieces(2, mark) + [first, second], coulombs[2], matrices)
    sums.append(core_sum(part, (True, True)))
    place, *sums[2] = lax.optimization_barrier((place, *sums[2]))
    place, part = call(place, pieces(3, mark) + [first, second], coulombs[2], matrices)
    sums.append(core_sum(part, (False, True)))
    terms = []
    for (dy, dx), both in zip(orders, sums):
        for dz in range(2):
            if (dy, dx, dz) == (0, 0, 0):
                terms.append(both[dz])
            else:
                arrived = receive(both[dz], offset_source(dy, dx, dz, 0))
                terms.append(arrived.astype(f32))
    return -sum(terms[1:], terms[0])[None]


def solution(mesh):
    in_specs = (P("tgt", "grp", None, None), P("tgt", None, None, None), P(), P(), P())
    out_specs = P("tgt", "grp", None, None)

    return jax.shard_map(body, mesh=mesh, in_specs=in_specs, out_specs=out_specs, check_vma=False)
```

```python
import functools
import math

import jax
import jax.numpy as jnp
import numpy as np
from jax import lax
from jax.experimental import pallas as pl
from jax.experimental.pallas import tpu as pltpu
from jax.sharding import PartitionSpec as P


coulomb_scale = 0.1
points = 64
lanes = 2 * points
quarter = 16
splits = 4
pitch = 72
axes = ("tgt", "grp")
f32 = jnp.float32
bf16 = jnp.bfloat16


devices = [
    (zh, y, x, zl, c)
    for zh in range(2)
    for y in range(4)
    for x in range(4)
    for zl in range(2)
    for c in range(2)
]
number = {device: i for i, device in enumerate(devices)}


def outer(i):
    return (i + 3) % 4 if i % 2 == 0 else (i + 1) % 4


def first_source(zh, y, x, zl, c):
    return {
        (0, 0): (zh, y, x, 0, 1),
        (0, 1): (zh ^ 1, y, x, 1, 0),
        (1, 0): (zh, outer(y), x, 1, 1),
        (1, 1): (zh ^ 1, y, outer(x), 0, 0),
    }[zl, c]


def second_source(zh, y, x, zl, c):
    return {
        (0, 0): (zh, outer(y), outer(x), 0, 1),
        (0, 1): (zh ^ 1, outer(y), outer(x), 1, 0),
        (1, 0): (zh, y, outer(x), 1, 1),
        (1, 1): (zh ^ 1, outer(y), x, 0, 0),
    }[zl, c]


def offset_source(dy, dx, dz, dc):
    return lambda zh, y, x, zl, c: (zh, y ^ dy, x ^ dx, zl ^ dz, c ^ dc)


def receive(value, source):
    pairs = [(number[source(*device)], number[device]) for device in devices]
    return lax.ppermute(value, axes, pairs)


def slot_table():
    slot = lambda d: (d[0] * 4 + d[1]) * 4 + d[2]
    return np.array(
        [[slot(first_source(*d)), slot(second_source(*d))] for d in devices], np.int32
    )


def tables():
    indices = np.arange(points)
    phases = indices[:, None] * indices[None, :] % points
    angles = phases.astype(np.float32) * np.float32(2.0 * math.pi / points)
    scale = np.float32(1.0 / math.sqrt(points))
    rounded = lambda t: (t * scale).astype(bf16).astype(np.float32)
    return rounded(np.cos(angles)), rounded(np.sin(angles))


def section_matrices():
    cosine, sine = tables()
    both = lambda t: np.kron(np.eye(2, dtype=np.float32), t)
    left_forward = np.block([[cosine, sine], [-sine, cosine]])
    left_inverse = np.block([[cosine, -sine], [sine, cosine]])
    right_forward = np.block([[both(cosine), both(-sine)], [both(sine), both(cosine)]])
    right_inverse = np.block([[both(cosine), both(sine)], [both(-sine), both(cosine)]])
    return [
        jnp.asarray(m, bf16) for m in (left_forward, left_inverse, right_forward, right_inverse)
    ]


def pair_weights(occupations, slot_partner, slots):
    ids = jnp.arange(occupations.shape[0], dtype=jnp.int32)
    match = slot_partner[:, None] == ids[None, :]
    by_slot = jnp.sum(jnp.where(match, occupations[None, :], 0.0), axis=1)
    return jnp.sum(jnp.where(slots[:, None] == ids[None, :], by_slot[None, :], 0.0), axis=1)


def coulomb_kernel(screening, weights):
    indices = jnp.arange(points, dtype=jnp.int32)
    signed = jnp.where(indices < points // 2, indices, indices - points).astype(f32) * (
        2.0 * math.pi / points
    )
    squares = signed * signed
    wave_sq = squares[:, None, None] + squares[None, :, None] + jnp.tile(squares, 2)[None, None, :]
    screen_wave = screening[0] * (2.0 * math.pi / points)
    lane = jnp.arange(lanes, dtype=jnp.int32)
    weight = jnp.where(lane < points, weights[0], weights[1])
    return (coulomb_scale / (wave_sq + screen_wave * screen_wave)) * weight[None, None, :]


def pair_kernel(two_targets, stage, *refs):
    refs = list(refs)
    take = lambda count: [refs.pop(0) for _ in range(count)]
    (place_ref,) = take(1)
    if two_targets:
        targets = [take(4), take(4)]
        (shared,) = take(1)
    else:
        shared = take(4)
        partners = take(2)
    coulomb, lf_ref, li_ref, rf_ref, ri_ref = take(5)
    earlier = take(2) if stage == "last" else []
    outs = take(2)
    results_count = 2 if two_targets else 1
    x_v, a_v, b_v, k_v, s_ref, z_ref, y_ref, o_v, e_v, in_sem, k_sem, e_sem, out_sem = refs

    dot = functools.partial(jnp.dot, preferred_element_type=f32)
    place = place_ref[0]
    rows = quarter * points
    low = lax.broadcasted_iota(jnp.int16, (rows, lanes), 1) < points

    def block_of(step):
        return place ^ step

    def fetches(step, n):
        planes = pl.ds(block_of(step) * quarter, quarter)
        if two_targets:
            sources = [shared.at[planes], targets[0][n], targets[1][n]]
        else:
            sources = [shared[n], partners[0].at[planes], partners[1].at[planes]]
        return [
            pltpu.make_async_copy(source, v.at[step], in_sem.at[step, i])
            for i, (source, v) in enumerate(zip(sources, (x_v, a_v, b_v)))
        ]

    for step in range(4):
        for copy in fetches(step, step):
            copy.start()
    k_copy = pltpu.make_async_copy(coulomb, k_v, k_sem)
    k_copy.start()
    e_copies = [
        pltpu.make_async_copy(source, e_v.at[dc], e_sem.at[dc]) for dc, source in enumerate(earlier)
    ]
    for copy in e_copies:
        copy.start()
    lf = lf_ref[...]
    li = li_ref[...]

    def load(ref, step):
        return ref[step].reshape(rows, lanes)

    def swap(v):
        return pltpu.roll(v, points, 1)

    def planes_of(v):
        return v.reshape(quarter, points, lanes)

    def last_section(field, matrix):
        part = rows // splits
        parts = [dot(field[n * part : (n + 1) * part], matrix).astype(bf16) for n in range(splits)]
        return jnp.concatenate(parts, axis=0)

    def arrive(step):
        for copy in fetches(step, 0):
            copy.wait()

    def forward_z(step):
        x = load(x_v, step)
        swapped = swap(x)
        x_real = jnp.where(low, x, swapped)
        x_imag = jnp.where(low, swapped, x)
        a = load(a_v, step)
        b = load(b_v, step)
        q_real = jnp.where(low, a, swap(b))
        q_imag = jnp.where(low, swap(a), b)
        p_real, p_imag = (x_real, x_imag) if two_targets else (q_real, q_imag)
        t_real, t_imag = (q_real, q_imag) if two_targets else (x_real, x_imag)
        a_v[step] = planes_of(p_real)
        b_v[step] = planes_of(p_imag)
        density = jnp.concatenate(
            [p_real * t_real + p_imag * t_imag, p_real * t_imag - p_imag * t_real], axis=1
        )
        along_z = last_section(density, rf_ref[...])
        slot = step % 2
        for j in range(quarter):
            for c in range(2):
                z_ref[slot, j, c * points : (c + 1) * points] = along_z[
                    j * points : (j + 1) * points, c * lanes : (c + 1) * lanes
                ]

    def forward_y(step):
        slot = step % 2
        plane = block_of(step) * quarter
        along_y = dot(lf, jnp.concatenate([z_ref[slot, j] for j in range(quarter)], axis=1))
        for j in range(quarter):
            s_ref[pl.ds(plane + j, lanes, stride=pitch), :] = along_y[:, j * lanes : (j + 1) * lanes]

    def forward(step, carry):
        arrive(step + 1)
        forward_y(step)
        forward_z(step + 1)
        return carry

    arrive(0)
    forward_z(0)
    lax.fori_loop(0, 3, forward, 0)
    forward_y(3)
    k_copy.wait()

    def line(k, part):
        return pl.ds(pl.multiple_of((part * points + k) * pitch, 8), points)

    def middle(i, carry):
        first = i * quarter
        columns = []
        for j in range(quarter):
            parts = [s_ref[line(first + j, part), :].astype(bf16) for part in range(2)]
            columns.append(jnp.concatenate(parts, axis=0))
        spectrum = dot(lf, jnp.concatenate(columns, axis=1))
        weights = jnp.concatenate([k_v[first + j] for j in range(quarter)], axis=1)
        scaled = (spectrum * jnp.concatenate([weights, weights], axis=0)).astype(bf16)
        along_x = dot(li, scaled)
        for j in range(quarter):
            for part in range(2):
                s_ref[line(first + j, part), :] = along_x[
                    part * points : (part + 1) * points, j * lanes : (j + 1) * lanes
                ]
        return carry

    lax.fori_loop(0, 4, middle, 0)
    for copy in e_copies:
        copy.wait()

    def put(step, dc):
        return [
            pltpu.make_async_copy(
                o_v.at[i, step], outs[dc].at[i, step // 2], out_sem.at[i, step]
            )
            for i in range(results_count)
        ]

    def inverse_y(step):
        slot = step % 2
        plane = block_of(step) * quarter
        columns = [
            s_ref[pl.ds(plane + j, lanes, stride=pitch), :].astype(bf16) for j in range(quarter)
        ]
        along_y = dot(li, jnp.concatenate(columns, axis=1)).astype(bf16)
        for j in range(quarter):
            for c in range(2):
                y_ref[slot, j * points : (j + 1) * points, c * lanes : (c + 1) * lanes] = along_y[
                    c * points : (c + 1) * points, j * lanes : (j + 1) * lanes
                ]

    def inverse_z(step):
        potential = last_section(y_ref[step % 2], ri_ref[...])
        v_real = potential[:, :lanes]
        v_imag = potential[:, lanes:]
        p_real = load(a_v, step)
        p_imag = load(b_v, step)
        real = v_real * p_real - v_imag * p_imag
        imag = v_real * p_imag + v_imag * p_real
        if stage == "first":
            results = [real, imag]
        elif stage == "last":
            real = real + e_v[step % 2, 0, step // 2].reshape(rows, lanes)
            imag = imag + e_v[step % 2, 1, step // 2].reshape(rows, lanes)
            results = [jnp.where(low, real, swap(imag)), jnp.where(low, swap(real), imag)]
        else:
            results = [jnp.where(low, real, imag) + swap(jnp.where(low, imag, real))]
        for i, result in enumerate(results):
            o_v[i, step] = planes_of(result)

    def inverse(step, carry):
        inverse_z(step)
        inverse_y(step + 1)
        for dc in range(2):

            @pl.when(step % 2 == dc)
            def _():
                for copy in put(step, dc):
                    copy.start()

        return carry

    inverse_y(0)
    lax.fori_loop(0, 3, inverse, 0)
    inverse_z(3)
    for copy in put(3, 1):
        copy.start()
    for step in range(4):
        for copy in put(step, step % 2):
            copy.wait()


def exchange_part(place, sides, coulomb, matrices, two_targets=False, stage="only", earlier=()):
    anywhere = pl.BlockSpec(memory_space=pl.ANY)
    scalar = pl.BlockSpec(memory_space=pltpu.SMEM)
    near = pl.BlockSpec(memory_space=pltpu.VMEM)
    planes = (4, quarter, points, lanes)
    results = 2 if two_targets else 1
    halves = (results, 2, quarter, points, lanes)
    return pl.pallas_call(
        functools.partial(pair_kernel, two_targets, stage),
        out_shape=[jax.ShapeDtypeStruct(halves, bf16)] * 2,
        in_specs=[scalar]
        + [anywhere] * (len(sides) + 1)
        + [near] * 4
        + [anywhere] * len(earlier),
        out_specs=[anywhere] * 2,
        scratch_shapes=[
            pltpu.VMEM(planes, bf16),
            pltpu.VMEM(planes, bf16),
            pltpu.VMEM(planes, bf16),
            pltpu.VMEM((points, points, lanes), f32),
            pltpu.VMEM((2 * points * pitch, lanes), f32),
            pltpu.VMEM((2, quarter, lanes, lanes), bf16),
            pltpu.VMEM((2, quarter * points, 2 * lanes), bf16),
            pltpu.VMEM((results, *planes), bf16),
            pltpu.VMEM((2, *halves), bf16),
            pltpu.SemaphoreType.DMA((4, 3)),
            pltpu.SemaphoreType.DMA,
            pltpu.SemaphoreType.DMA((2,)),
            pltpu.SemaphoreType.DMA((2, 4)),
        ],
        compiler_params=pltpu.CompilerParams(vmem_limit_bytes=40 << 20),
        cost_estimate=pl.CostEstimate(
            flops=5 * 10**9, bytes_accessed=24 * 2**20, transcendentals=0
        ),
    )(place, *sides, coulomb, *matrices, *earlier)


def body(targets, partners, occupations, slot_partner, screening):
    own = targets[0]
    partner = partners[0]
    first = receive(partner, first_source)
    orders = [(0, 1), (1, 0), (1, 1), (0, 0)]
    halves = []
    sent = own
    for n, (dy, dx) in enumerate(orders):
        if n == 2:
            sent, *halves[1] = lax.optimization_barrier((own, *halves[1]))
        half = []
        for dz in range(2):
            source = offset_source(dy, dx, dz, 0)
            half.append(own if (dy, dx) == (0, 0) else receive(sent, source))
        halves.append(half)
    second = receive(partner, second_source)
    matrices = section_matrices()
    device = lax.axis_index("tgt") * 4 + lax.axis_index("grp")
    slots = lax.dynamic_slice_in_dim(jnp.asarray(slot_table()), device, 1)[0]
    place = lax.axis_index("grp")[None].astype(jnp.int32)
    weights = pair_weights(occupations, slot_partner, slots)
    sibling = offset_source(0, 0, 0, 1)

    def pieces(n, mark=None):
        same, other = halves[n]
        if mark is not None:
            _, same, other = lax.optimization_barrier((mark, same, other))
        crossed = []
        for piece in (same, other):
            crossed.append(receive(piece, sibling))
        return [same, crossed[0], other, crossed[1]]

    def core_sum(kept, given, rounded):
        both = []
        for dz in range(2):
            crossed = receive(given[dz], sibling)
            summed = kept[dz].astype(f32) + crossed.astype(f32)
            both.append(summed.astype(bf16) if rounded[dz] else summed)
        return both

    def call(place, *args, **kwargs):
        parts = exchange_part(place, *args, **kwargs)
        return lax.optimization_barrier((place, *parts))

    coulombs = [
        coulomb_kernel(screening, (weights[a], weights[b])) for a, b in ((0, 0), (1, 1), (0, 1))
    ]
    *coulombs, halves[0][1], halves[1][1] = lax.optimization_barrier(
        (*coulombs, halves[0][1], halves[1][1])
    )
    two = pieces(0) + pieces(1)
    place, *earlier = call(
        place, two + [first], coulombs[0], matrices, two_targets=True, stage="first"
    )
    mark = place
    _, sent = lax.optimization_barrier((mark, own))
    halves[3][1] = receive(sent, offset_source(0, 0, 1, 0))
    place, kept, given = call(place, two + [second], coulombs[1], matrices, True, "last", earlier)
    crossed = receive(given, sibling)
    place, kept_2, given_2 = call(place, pieces(2, mark) + [first, second], coulombs[2], matrices)
    summed = (kept.astype(f32) + crossed.astype(f32)).astype(bf16)
    sums = [[summed[n, dz] for dz in range(2)] for n in range(2)]
    sums.append(core_sum(kept_2[0], given_2[0], (True, True)))
    place, *flat = lax.optimization_barrier((place, *sums[0], *sums[1]))
    sums[:2] = [flat[:2], flat[2:]]
    place, kept, given = call(place, pieces(3, mark) + [first, second], coulombs[2], matrices)
    sums.append(core_sum(kept[0], given[0], (False, True)))
    terms = []
    for (dy, dx), both in zip(orders, sums):
        for dz in range(2):
            if (dy, dx, dz) == (0, 0, 0):
                terms.append(both[dz])
            else:
                arrived = receive(both[dz], offset_source(dy, dx, dz, 0))
                terms.append(arrived.astype(f32))
    return -sum(terms[1:], terms[0])[None]


def solution(mesh):
    in_specs = (P("tgt", "grp", None, None), P("tgt", None, None, None), P(), P(), P())
    out_specs = P("tgt", "grp", None, None)

    return jax.shard_map(body, mesh=mesh, in_specs=in_specs, out_specs=out_specs, check_vma=False)
```

```python
import functools
import math

import jax
import jax.numpy as jnp
import numpy as np
from jax import lax
from jax.experimental import pallas as pl
from jax.experimental.pallas import tpu as pltpu
from jax.sharding import PartitionSpec as P


coulomb_scale = 0.1
points = 64
lanes = 2 * points
quarter = 16
splits = 4
pitch = 72
axes = ("tgt", "grp")
f32 = jnp.float32
bf16 = jnp.bfloat16


devices = [
    (zh, y, x, zl, c)
    for zh in range(2)
    for y in range(4)
    for x in range(4)
    for zl in range(2)
    for c in range(2)
]
number = {device: i for i, device in enumerate(devices)}


def outer(i):
    return (i + 3) % 4 if i % 2 == 0 else (i + 1) % 4


def first_source(zh, y, x, zl, c):
    return {
        (0, 0): (zh, y, x, 0, 1),
        (0, 1): (zh ^ 1, y, x, 1, 0),
        (1, 0): (zh, outer(y), x, 1, 1),
        (1, 1): (zh ^ 1, y, outer(x), 0, 0),
    }[zl, c]


def second_source(zh, y, x, zl, c):
    return {
        (0, 0): (zh, outer(y), outer(x), 0, 1),
        (0, 1): (zh ^ 1, outer(y), outer(x), 1, 0),
        (1, 0): (zh, y, outer(x), 1, 1),
        (1, 1): (zh ^ 1, outer(y), x, 0, 0),
    }[zl, c]


def offset_source(dy, dx, dz, dc):
    return lambda zh, y, x, zl, c: (zh, y ^ dy, x ^ dx, zl ^ dz, c ^ dc)


def receive(value, source):
    pairs = [(number[source(*device)], number[device]) for device in devices]
    return lax.ppermute(value, axes, pairs)


def slot_table():
    slot = lambda d: (d[0] * 4 + d[1]) * 4 + d[2]
    return np.array(
        [[slot(first_source(*d)), slot(second_source(*d))] for d in devices], np.int32
    )


def tables():
    indices = np.arange(points)
    phases = indices[:, None] * indices[None, :] % points
    angles = phases.astype(np.float32) * np.float32(2.0 * math.pi / points)
    scale = np.float32(1.0 / math.sqrt(points))
    rounded = lambda t: (t * scale).astype(bf16).astype(np.float32)
    return rounded(np.cos(angles)), rounded(np.sin(angles))


def section_matrices():
    cosine, sine = tables()
    both = lambda t: np.kron(np.eye(2, dtype=np.float32), t)
    left_forward = np.block([[cosine, sine], [-sine, cosine]])
    left_inverse = np.block([[cosine, -sine], [sine, cosine]])
    right_forward = np.block([[both(cosine), both(-sine)], [both(sine), both(cosine)]])
    right_inverse = np.block([[both(cosine), both(sine)], [both(-sine), both(cosine)]])
    return [
        jnp.asarray(m, bf16) for m in (left_forward, left_inverse, right_forward, right_inverse)
    ]


def pair_weights(occupations, slot_partner, slots):
    ids = jnp.arange(occupations.shape[0], dtype=jnp.int32)
    match = slot_partner[:, None] == ids[None, :]
    by_slot = jnp.sum(jnp.where(match, occupations[None, :], 0.0), axis=1)
    return jnp.sum(jnp.where(slots[:, None] == ids[None, :], by_slot[None, :], 0.0), axis=1)


def coulomb_kernel(screening, weights):
    indices = jnp.arange(points, dtype=jnp.int32)
    signed = jnp.where(indices < points // 2, indices, indices - points).astype(f32) * (
        2.0 * math.pi / points
    )
    squares = signed * signed
    wave_sq = squares[:, None, None] + squares[None, :, None] + jnp.tile(squares, 2)[None, None, :]
    screen_wave = screening[0] * (2.0 * math.pi / points)
    lane = jnp.arange(lanes, dtype=jnp.int32)
    weight = jnp.where(lane < points, weights[0], weights[1])
    return (coulomb_scale / (wave_sq + screen_wave * screen_wave)) * weight[None, None, :]


def pair_kernel(two_targets, stage, *refs):
    refs = list(refs)
    take = lambda count: [refs.pop(0) for _ in range(count)]
    (place_ref,) = take(1)
    if two_targets:
        targets = [take(4), take(4)]
        (shared,) = take(1)
    else:
        shared = take(4)
        partners = take(2)
    coulomb, lf_ref, li_ref, rf_ref, ri_ref = take(5)
    earlier = take(2) if stage == "last" else []
    outs = take(2)
    results_count = 2 if two_targets else 1
    x_v, a_v, b_v, k_v, s_ref, z_ref, y_ref, o_v, e_v, in_sem, k_sem, e_sem, out_sem = refs

    dot = functools.partial(jnp.dot, preferred_element_type=f32)
    place = place_ref[0]
    rows = quarter * points
    low = lax.broadcasted_iota(jnp.int16, (rows, lanes), 1) < points

    def block_of(step):
        return place ^ step

    def fetches(step, n):
        planes = pl.ds(block_of(step) * quarter, quarter)
        if two_targets:
            sources = [shared.at[planes], targets[0][n], targets[1][n]]
        else:
            sources = [shared[n], partners[0].at[planes], partners[1].at[planes]]
        return [
            pltpu.make_async_copy(source, v.at[step], in_sem.at[step, i])
            for i, (source, v) in enumerate(zip(sources, (x_v, a_v, b_v)))
        ]

    for step in range(4):
        for copy in fetches(step, step):
            copy.start()
    k_copy = pltpu.make_async_copy(coulomb, k_v, k_sem)
    k_copy.start()
    e_copies = [
        pltpu.make_async_copy(source, e_v.at[dc], e_sem.at[dc]) for dc, source in enumerate(earlier)
    ]
    for copy in e_copies:
        copy.start()
    lf = lf_ref[...]
    li = li_ref[...]

    def load(ref, step):
        return ref[step].reshape(rows, lanes)

    def swap(v):
        return pltpu.roll(v, points, 1)

    def planes_of(v):
        return v.reshape(quarter, points, lanes)

    def last_section(field, matrix):
        part = rows // splits
        parts = [dot(field[n * part : (n + 1) * part], matrix).astype(bf16) for n in range(splits)]
        return jnp.concatenate(parts, axis=0)

    def arrive(step):
        for copy in fetches(step, 0):
            copy.wait()

    def forward_z(step):
        x = load(x_v, step)
        swapped = swap(x)
        x_real = jnp.where(low, x, swapped)
        x_imag = jnp.where(low, swapped, x)
        a = load(a_v, step)
        b = load(b_v, step)
        q_real = jnp.where(low, a, swap(b))
        q_imag = jnp.where(low, swap(a), b)
        p_real, p_imag = (x_real, x_imag) if two_targets else (q_real, q_imag)
        t_real, t_imag = (q_real, q_imag) if two_targets else (x_real, x_imag)
        a_v[step] = planes_of(p_real)
        b_v[step] = planes_of(p_imag)
        density = jnp.concatenate(
            [p_real * t_real + p_imag * t_imag, p_real * t_imag - p_imag * t_real], axis=1
        )
        along_z = last_section(density, rf_ref[...])
        slot = step % 2
        for j in range(quarter):
            for c in range(2):
                z_ref[slot, j, c * points : (c + 1) * points] = along_z[
                    j * points : (j + 1) * points, c * lanes : (c + 1) * lanes
                ]

    def forward_y(step):
        slot = step % 2
        plane = block_of(step) * quarter
        along_y = dot(lf, jnp.concatenate([z_ref[slot, j] for j in range(quarter)], axis=1))
        for j in range(quarter):
            s_ref[pl.ds(plane + j, lanes, stride=pitch), :] = along_y[:, j * lanes : (j + 1) * lanes]

    def forward(step, carry):
        arrive(step + 1)
        forward_y(step)
        forward_z(step + 1)
        return carry

    arrive(0)
    forward_z(0)
    lax.fori_loop(0, 3, forward, 0)
    forward_y(3)
    k_copy.wait()

    def line(k, part):
        return pl.ds(pl.multiple_of((part * points + k) * pitch, 8), points)

    def middle(i, carry):
        first = i * quarter
        columns = []
        for j in range(quarter):
            parts = [s_ref[line(first + j, part), :].astype(bf16) for part in range(2)]
            columns.append(jnp.concatenate(parts, axis=0))
        spectrum = dot(lf, jnp.concatenate(columns, axis=1))
        weights = jnp.concatenate([k_v[first + j] for j in range(quarter)], axis=1)
        scaled = (spectrum * jnp.concatenate([weights, weights], axis=0)).astype(bf16)
        along_x = dot(li, scaled)
        for j in range(quarter):
            for part in range(2):
                s_ref[line(first + j, part), :] = along_x[
                    part * points : (part + 1) * points, j * lanes : (j + 1) * lanes
                ]
        return carry

    lax.fori_loop(0, 4, middle, 0)
    for copy in e_copies:
        copy.wait()

    def put(step, dc):
        return [
            pltpu.make_async_copy(
                o_v.at[i, step], outs[dc].at[i, step // 2], out_sem.at[i, step]
            )
            for i in range(results_count)
        ]

    def inverse_y(step):
        slot = step % 2
        plane = block_of(step) * quarter
        columns = [
            s_ref[pl.ds(plane + j, lanes, stride=pitch), :].astype(bf16) for j in range(quarter)
        ]
        along_y = dot(li, jnp.concatenate(columns, axis=1)).astype(bf16)
        for j in range(quarter):
            for c in range(2):
                y_ref[slot, j * points : (j + 1) * points, c * lanes : (c + 1) * lanes] = along_y[
                    c * points : (c + 1) * points, j * lanes : (j + 1) * lanes
                ]

    def inverse_z(step):
        potential = last_section(y_ref[step % 2], ri_ref[...])
        v_real = potential[:, :lanes]
        v_imag = potential[:, lanes:]
        p_real = load(a_v, step)
        p_imag = load(b_v, step)
        real = v_real * p_real - v_imag * p_imag
        imag = v_real * p_imag + v_imag * p_real
        if stage == "first":
            results = [real, imag]
        elif stage == "last":
            real = real + e_v[step % 2, 0, step // 2].reshape(rows, lanes)
            imag = imag + e_v[step % 2, 1, step // 2].reshape(rows, lanes)
            results = [jnp.where(low, real, swap(imag)), jnp.where(low, swap(real), imag)]
        else:
            results = [jnp.where(low, real, imag) + swap(jnp.where(low, imag, real))]
        for i, result in enumerate(results):
            o_v[i, step] = planes_of(result)

    def inverse(step, carry):
        inverse_z(step)
        inverse_y(step + 1)
        for dc in range(2):

            @pl.when(step % 2 == dc)
            def _():
                for copy in put(step, dc):
                    copy.start()

        return carry

    inverse_y(0)
    lax.fori_loop(0, 3, inverse, 0)
    inverse_z(3)
    for copy in put(3, 1):
        copy.start()
    for step in range(4):
        for copy in put(step, step % 2):
            copy.wait()


def exchange_part(place, sides, coulomb, matrices, two_targets=False, stage="only", earlier=()):
    anywhere = pl.BlockSpec(memory_space=pl.ANY)
    scalar = pl.BlockSpec(memory_space=pltpu.SMEM)
    near = pl.BlockSpec(memory_space=pltpu.VMEM)
    planes = (4, quarter, points, lanes)
    results = 2 if two_targets else 1
    halves = (results, 2, quarter, points, lanes)
    return pl.pallas_call(
        functools.partial(pair_kernel, two_targets, stage),
        out_shape=[jax.ShapeDtypeStruct(halves, bf16)] * 2,
        in_specs=[scalar]
        + [anywhere] * (len(sides) + 1)
        + [near] * 4
        + [anywhere] * len(earlier),
        out_specs=[anywhere] * 2,
        scratch_shapes=[
            pltpu.VMEM(planes, bf16),
            pltpu.VMEM(planes, bf16),
            pltpu.VMEM(planes, bf16),
            pltpu.VMEM((points, points, lanes), f32),
            pltpu.VMEM((2 * points * pitch, lanes), f32),
            pltpu.VMEM((2, quarter, lanes, lanes), bf16),
            pltpu.VMEM((2, quarter * points, 2 * lanes), bf16),
            pltpu.VMEM((results, *planes), bf16),
            pltpu.VMEM((2, *halves), bf16),
            pltpu.SemaphoreType.DMA((4, 3)),
            pltpu.SemaphoreType.DMA,
            pltpu.SemaphoreType.DMA((2,)),
            pltpu.SemaphoreType.DMA((2, 4)),
        ],
        compiler_params=pltpu.CompilerParams(vmem_limit_bytes=40 << 20),
        cost_estimate=pl.CostEstimate(
            flops=5 * 10**9, bytes_accessed=24 * 2**20, transcendentals=0
        ),
    )(place, *sides, coulomb, *matrices, *earlier)


def body(targets, partners, occupations, slot_partner, screening):
    own = targets[0]
    partner = partners[0]
    first = receive(partner, first_source)
    orders = [(0, 1), (1, 0), (1, 1), (0, 0)]
    halves = []
    sent = own
    for n, (dy, dx) in enumerate(orders):
        if n == 2:
            sent, *halves[1] = lax.optimization_barrier((own, *halves[1]))
        half = []
        for dz in range(2):
            source = offset_source(dy, dx, dz, 0)
            half.append(own if (dy, dx) == (0, 0) else receive(sent, source))
        halves.append(half)
    second = receive(partner, second_source)
    matrices = section_matrices()
    device = lax.axis_index("tgt") * 4 + lax.axis_index("grp")
    slots = lax.dynamic_slice_in_dim(jnp.asarray(slot_table()), device, 1)[0]
    place = lax.axis_index("grp")[None].astype(jnp.int32)
    weights = pair_weights(occupations, slot_partner, slots)
    sibling = offset_source(0, 0, 0, 1)

    def pieces(n, mark=None):
        same, other = halves[n]
        if mark is not None:
            _, same, other = lax.optimization_barrier((mark, same, other))
        crossed = []
        for piece in (same, other):
            crossed.append(receive(piece, sibling))
        return [same, crossed[0], other, crossed[1]]

    def core_sum(kept, given, rounded):
        both = []
        for dz in range(2):
            crossed = receive(given[dz], sibling)
            summed = kept[dz].astype(f32) + crossed.astype(f32)
            both.append(summed.astype(bf16) if rounded[dz] else summed)
        return both

    def call(place, *args, **kwargs):
        parts = exchange_part(place, *args, **kwargs)
        return lax.optimization_barrier((place, *parts))

    coulombs = [
        coulomb_kernel(screening, (weights[a], weights[b])) for a, b in ((0, 0), (1, 1), (0, 1))
    ]
    *coulombs, halves[0][1], halves[1][1] = lax.optimization_barrier(
        (*coulombs, halves[0][1], halves[1][1])
    )
    two = pieces(0) + pieces(1)
    place, *earlier = call(
        place, two + [first], coulombs[0], matrices, two_targets=True, stage="first"
    )
    mark = place
    _, sent = lax.optimization_barrier((mark, own))
    halves[3][1] = receive(sent, offset_source(0, 0, 1, 0))
    place, kept, given = call(place, two + [second], coulombs[1], matrices, True, "last", earlier)
    crossed = receive(given, sibling)
    summed = (kept.astype(f32) + crossed.astype(f32)).astype(bf16)
    sums = [[summed[n, dz] for dz in range(2)] for n in range(2)]
    place, *flat = lax.optimization_barrier((place, *sums[0], *sums[1]))
    sums[:2] = [flat[:2], flat[2:]]
    place, kept, given = call(place, pieces(2, mark) + [first, second], coulombs[2], matrices)
    sums.append(core_sum(kept[0], given[0], (True, True)))
    place, *sums[2] = lax.optimization_barrier((place, *sums[2]))
    place, kept, given = call(place, pieces(3, mark) + [first, second], coulombs[2], matrices)
    crossed = receive(given[0, 1], sibling)
    crossed_0 = receive(given[0, 0], sibling)
    leaving = (kept[0, 1].astype(f32) + crossed.astype(f32)).astype(bf16)
    leaving, kept_0 = lax.optimization_barrier((leaving, kept[0, 0]))
    sums.append([kept_0.astype(f32) + crossed_0.astype(f32), leaving])
    arrived = {}
    for n, ((dy, dx), both) in enumerate(zip(orders, sums)):
        for dz in range(2):
            if (dy, dx, dz) != (0, 0, 0):
                arrived[n, dz] = receive(both[dz], offset_source(dy, dx, dz, 0)).astype(f32)
    early = sum((arrived[n, dz] for n in range(3) for dz in range(2)), sums[3][0])
    early = lax.optimization_barrier(early)
    return -(early + arrived[3, 1])[None]


def solution(mesh):
    in_specs = (P("tgt", "grp", None, None), P("tgt", None, None, None), P(), P(), P())
    out_specs = P("tgt", "grp", None, None)

    return jax.shard_map(body, mesh=mesh, in_specs=in_specs, out_specs=out_specs, check_vma=False)
```

```python
import functools
import math

import jax
import jax.numpy as jnp
import numpy as np
from jax import lax
from jax.experimental import pallas as pl
from jax.experimental.pallas import tpu as pltpu
from jax.sharding import PartitionSpec as P


coulomb_scale = 0.1
points = 64
lanes = 2 * points
quarter = 16
splits = 4
pitch = 72
axes = ("tgt", "grp")
f32 = jnp.float32
bf16 = jnp.bfloat16


devices = [
    (zh, y, x, zl, c)
    for zh in range(2)
    for y in range(4)
    for x in range(4)
    for zl in range(2)
    for c in range(2)
]
number = {device: i for i, device in enumerate(devices)}


def outer(i):
    return (i + 3) % 4 if i % 2 == 0 else (i + 1) % 4


def first_source(zh, y, x, zl, c):
    return {
        (0, 0): (zh, y, outer(x), 0, 0),
        (0, 1): (zh ^ 1, outer(y), outer(x), 1, 0),
        (1, 0): (zh, y, x, 1, 1),
        (1, 1): (zh ^ 1, outer(y), x, 0, 1),
    }[zl, c]


def second_source(zh, y, x, zl, c):
    return {
        (0, 0): (zh, outer(y), outer(x), 0, 0),
        (0, 1): (zh ^ 1, y, outer(x), 1, 0),
        (1, 0): (zh, outer(y), x, 1, 1),
        (1, 1): (zh ^ 1, y, x, 0, 1),
    }[zl, c]


def offset_source(dy, dx, dz, dc):
    return lambda zh, y, x, zl, c: (zh, y ^ dy, x ^ dx, zl ^ dz, c ^ dc)


def receive(value, source):
    pairs = [(number[source(*device)], number[device]) for device in devices]
    return lax.ppermute(value, axes, pairs)


def slot_table():
    slot = lambda d: (d[0] * 4 + d[1]) * 4 + d[2]
    return np.array(
        [[slot(first_source(*d)), slot(second_source(*d))] for d in devices], np.int32
    )


def tables():
    indices = np.arange(points)
    phases = indices[:, None] * indices[None, :] % points
    angles = phases.astype(np.float32) * np.float32(2.0 * math.pi / points)
    scale = np.float32(1.0 / math.sqrt(points))
    rounded = lambda t: (t * scale).astype(bf16).astype(np.float32)
    return rounded(np.cos(angles)), rounded(np.sin(angles))


def section_matrices():
    cosine, sine = tables()
    both = lambda t: np.kron(np.eye(2, dtype=np.float32), t)
    left_forward = np.block([[cosine, sine], [-sine, cosine]])
    left_inverse = np.block([[cosine, -sine], [sine, cosine]])
    right_forward = np.block([[both(cosine), both(-sine)], [both(sine), both(cosine)]])
    right_inverse = np.block([[both(cosine), both(sine)], [both(-sine), both(cosine)]])
    return [
        jnp.asarray(m, bf16) for m in (left_forward, left_inverse, right_forward, right_inverse)
    ]


def pair_weights(occupations, slot_partner, slots):
    ids = jnp.arange(occupations.shape[0], dtype=jnp.int32)
    match = slot_partner[:, None] == ids[None, :]
    by_slot = jnp.sum(jnp.where(match, occupations[None, :], 0.0), axis=1)
    return jnp.sum(jnp.where(slots[:, None] == ids[None, :], by_slot[None, :], 0.0), axis=1)


def coulomb_kernel(screening, weights):
    indices = jnp.arange(points, dtype=jnp.int32)
    signed = jnp.where(indices < points // 2, indices, indices - points).astype(f32) * (
        2.0 * math.pi / points
    )
    squares = signed * signed
    wave_sq = squares[:, None, None] + squares[None, :, None] + jnp.tile(squares, 2)[None, None, :]
    screen_wave = screening[0] * (2.0 * math.pi / points)
    lane = jnp.arange(lanes, dtype=jnp.int32)
    weight = jnp.where(lane < points, weights[0], weights[1])
    return (coulomb_scale / (wave_sq + screen_wave * screen_wave)) * weight[None, None, :]


def pair_kernel(two_targets, stage, *refs):
    refs = list(refs)
    take = lambda count: [refs.pop(0) for _ in range(count)]
    (place_ref,) = take(1)
    if two_targets:
        targets = [take(4), take(4)]
        (shared,) = take(1)
    else:
        shared = take(4)
        partners = take(2)
    coulomb, lf_ref, li_ref, rf_ref, ri_ref = take(5)
    earlier = take(2) if stage == "last" else []
    outs = take(2)
    results_count = 2 if two_targets else 1
    x_v, a_v, b_v, k_v, s_ref, z_ref, y_ref, o_v, e_v, in_sem, k_sem, e_sem, out_sem = refs

    dot = functools.partial(jnp.dot, preferred_element_type=f32)
    place = place_ref[0]
    rows = quarter * points
    low = lax.broadcasted_iota(jnp.int16, (rows, lanes), 1) < points

    def block_of(step):
        return place ^ step

    def fetches(step, n):
        planes = pl.ds(block_of(step) * quarter, quarter)
        if two_targets:
            sources = [shared.at[planes], targets[0][n], targets[1][n]]
        else:
            sources = [shared[n], partners[0].at[planes], partners[1].at[planes]]
        return [
            pltpu.make_async_copy(source, v.at[step], in_sem.at[step, i])
            for i, (source, v) in enumerate(zip(sources, (x_v, a_v, b_v)))
        ]

    for step in range(4):
        for copy in fetches(step, step):
            copy.start()
    k_copy = pltpu.make_async_copy(coulomb, k_v, k_sem)
    k_copy.start()
    e_copies = [
        pltpu.make_async_copy(source, e_v.at[dc], e_sem.at[dc]) for dc, source in enumerate(earlier)
    ]
    for copy in e_copies:
        copy.start()
    lf = lf_ref[...]
    li = li_ref[...]

    def load(ref, step):
        return ref[step].reshape(rows, lanes)

    def swap(v):
        return pltpu.roll(v, points, 1)

    def planes_of(v):
        return v.reshape(quarter, points, lanes)

    def last_section(field, matrix):
        part = rows // splits
        parts = [dot(field[n * part : (n + 1) * part], matrix).astype(bf16) for n in range(splits)]
        return jnp.concatenate(parts, axis=0)

    def arrive(step):
        for copy in fetches(step, 0):
            copy.wait()

    def forward_z(step):
        x = load(x_v, step)
        swapped = swap(x)
        x_real = jnp.where(low, x, swapped)
        x_imag = jnp.where(low, swapped, x)
        a = load(a_v, step)
        b = load(b_v, step)
        q_real = jnp.where(low, a, swap(b))
        q_imag = jnp.where(low, swap(a), b)
        p_real, p_imag = (x_real, x_imag) if two_targets else (q_real, q_imag)
        t_real, t_imag = (q_real, q_imag) if two_targets else (x_real, x_imag)
        a_v[step] = planes_of(p_real)
        b_v[step] = planes_of(p_imag)
        density = jnp.concatenate(
            [p_real * t_real + p_imag * t_imag, p_real * t_imag - p_imag * t_real], axis=1
        )
        along_z = last_section(density, rf_ref[...])
        slot = step % 2
        for j in range(quarter):
            for c in range(2):
                z_ref[slot, j, c * points : (c + 1) * points] = along_z[
                    j * points : (j + 1) * points, c * lanes : (c + 1) * lanes
                ]

    def forward_y(step):
        slot = step % 2
        plane = block_of(step) * quarter
        along_y = dot(lf, jnp.concatenate([z_ref[slot, j] for j in range(quarter)], axis=1))
        for j in range(quarter):
            s_ref[pl.ds(plane + j, lanes, stride=pitch), :] = along_y[:, j * lanes : (j + 1) * lanes]

    arrive(0)
    forward_z(0)
    for step in range(3):
        arrive(step + 1)
    for step in range(3):
        forward_y(step)
        forward_z(step + 1)
    forward_y(3)
    k_copy.wait()

    def line(k, part):
        return pl.ds(pl.multiple_of((part * points + k) * pitch, 8), points)

    def middle(i, carry):
        first = i * quarter
        columns = []
        for j in range(quarter):
            parts = [s_ref[line(first + j, part), :].astype(bf16) for part in range(2)]
            columns.append(jnp.concatenate(parts, axis=0))
        spectrum = dot(lf, jnp.concatenate(columns, axis=1))
        weights = jnp.concatenate([k_v[first + j] for j in range(quarter)], axis=1)
        scaled = (spectrum * jnp.concatenate([weights, weights], axis=0)).astype(bf16)
        along_x = dot(li, scaled)
        for j in range(quarter):
            for part in range(2):
                s_ref[line(first + j, part), :] = along_x[
                    part * points : (part + 1) * points, j * lanes : (j + 1) * lanes
                ]
        return carry

    lax.fori_loop(0, 4, middle, 0)
    for copy in e_copies:
        copy.wait()

    def put(step, dc):
        return [
            pltpu.make_async_copy(
                o_v.at[i, step], outs[dc].at[i, step // 2], out_sem.at[i, step]
            )
            for i in range(results_count)
        ]

    def inverse_y(step):
        slot = step % 2
        plane = block_of(step) * quarter
        columns = [
            s_ref[pl.ds(plane + j, lanes, stride=pitch), :].astype(bf16) for j in range(quarter)
        ]
        along_y = dot(li, jnp.concatenate(columns, axis=1)).astype(bf16)
        for j in range(quarter):
            for c in range(2):
                y_ref[slot, j * points : (j + 1) * points, c * lanes : (c + 1) * lanes] = along_y[
                    c * points : (c + 1) * points, j * lanes : (j + 1) * lanes
                ]

    def inverse_z(step):
        potential = last_section(y_ref[step % 2], ri_ref[...])
        v_real = potential[:, :lanes]
        v_imag = potential[:, lanes:]
        p_real = load(a_v, step)
        p_imag = load(b_v, step)
        real = v_real * p_real - v_imag * p_imag
        imag = v_real * p_imag + v_imag * p_real
        if stage == "first":
            results = [real, imag]
        elif stage == "last":
            real = real + e_v[step % 2, 0, step // 2].reshape(rows, lanes)
            imag = imag + e_v[step % 2, 1, step // 2].reshape(rows, lanes)
            results = [jnp.where(low, real, swap(imag)), jnp.where(low, swap(real), imag)]
        else:
            results = [jnp.where(low, real, imag) + swap(jnp.where(low, imag, real))]
        for i, result in enumerate(results):
            o_v[i, step] = planes_of(result)

    def inverse(step, carry):
        inverse_z(step)
        inverse_y(step + 1)
        for dc in range(2):

            @pl.when(step % 2 == dc)
            def _():
                for copy in put(step, dc):
                    copy.start()

        return carry

    inverse_y(0)
    if stage == "last":
        lax.fori_loop(0, 3, inverse, 0)
    else:
        for step in range(3):
            inverse_z(step)
            inverse_y(step + 1)
    inverse_z(3)
    for step in range(3 if stage == "last" else 0, 4):
        for copy in put(step, step % 2):
            copy.start()
    for step in range(4):
        for copy in put(step, step % 2):
            copy.wait()


def exchange_part(place, sides, coulomb, matrices, two_targets=False, stage="only", earlier=()):
    anywhere = pl.BlockSpec(memory_space=pl.ANY)
    scalar = pl.BlockSpec(memory_space=pltpu.SMEM)
    near = pl.BlockSpec(memory_space=pltpu.VMEM)
    planes = (4, quarter, points, lanes)
    results = 2 if two_targets else 1
    halves = (results, 2, quarter, points, lanes)
    return pl.pallas_call(
        functools.partial(pair_kernel, two_targets, stage),
        out_shape=[jax.ShapeDtypeStruct(halves, bf16)] * 2,
        in_specs=[scalar]
        + [anywhere] * (len(sides) + 1)
        + [near] * 4
        + [anywhere] * len(earlier),
        out_specs=[anywhere] * 2,
        scratch_shapes=[
            pltpu.VMEM(planes, bf16),
            pltpu.VMEM(planes, bf16),
            pltpu.VMEM(planes, bf16),
            pltpu.VMEM((points, points, lanes), f32),
            pltpu.VMEM((2 * points * pitch, lanes), f32),
            pltpu.VMEM((2, quarter, lanes, lanes), bf16),
            pltpu.VMEM((2, quarter * points, 2 * lanes), bf16),
            pltpu.VMEM((results, *planes), bf16),
            pltpu.VMEM((2, *halves), bf16),
            pltpu.SemaphoreType.DMA((4, 3)),
            pltpu.SemaphoreType.DMA,
            pltpu.SemaphoreType.DMA((2,)),
            pltpu.SemaphoreType.DMA((2, 4)),
        ],
        compiler_params=pltpu.CompilerParams(vmem_limit_bytes=40 << 20),
        cost_estimate=pl.CostEstimate(
            flops=5 * 10**9, bytes_accessed=24 * 2**20, transcendentals=0
        ),
    )(place, *sides, coulomb, *matrices, *earlier)


def body(targets, partners, occupations, slot_partner, screening):
    own = targets[0]
    partner = partners[0]
    first = receive(partner, first_source)
    orders = [(0, 1), (1, 0), (1, 1), (0, 0)]
    halves = []
    sent = own
    for n, (dy, dx) in enumerate(orders):
        if n == 2:
            sent, *halves[1] = lax.optimization_barrier((own, *halves[1]))
        half = []
        for dz in range(2):
            source = offset_source(dy, dx, dz, 0)
            half.append(own if (dy, dx) == (0, 0) else receive(sent, source))
        halves.append(half)
    second = receive(partner, second_source)
    matrices = section_matrices()
    device = lax.axis_index("tgt") * 4 + lax.axis_index("grp")
    slots = lax.dynamic_slice_in_dim(jnp.asarray(slot_table()), device, 1)[0]
    place = lax.axis_index("grp")[None].astype(jnp.int32)
    weights = pair_weights(occupations, slot_partner, slots)
    sibling = offset_source(0, 0, 0, 1)

    def pieces(n, mark=None):
        same, other = halves[n]
        if mark is not None:
            _, same, other = lax.optimization_barrier((mark, same, other))
        crossed = []
        for piece in (same, other):
            crossed.append(receive(piece, sibling))
        return [same, crossed[0], other, crossed[1]]

    def core_sum(kept, given, rounded):
        both = []
        for dz in range(2):
            crossed = receive(given[dz], sibling)
            summed = kept[dz].astype(f32) + crossed.astype(f32)
            both.append(summed.astype(bf16) if rounded[dz] else summed)
        return both

    def call(place, *args, **kwargs):
        parts = exchange_part(place, *args, **kwargs)
        return lax.optimization_barrier((place, *parts))

    coulombs = [
        coulomb_kernel(screening, (weights[a], weights[b])) for a, b in ((0, 0), (1, 1), (0, 1))
    ]
    *coulombs, halves[0][1], halves[1][1] = lax.optimization_barrier(
        (*coulombs, halves[0][1], halves[1][1])
    )
    two = pieces(0) + pieces(1)
    place, *earlier = call(
        place, two + [first], coulombs[0], matrices, two_targets=True, stage="first"
    )
    mark = place
    _, sent = lax.optimization_barrier((mark, own))
    halves[3][1] = receive(sent, offset_source(0, 0, 1, 0))
    place, kept, given = call(place, two + [second], coulombs[1], matrices, True, "last", earlier)
    crossed = receive(given, sibling)
    summed = (kept.astype(f32) + crossed.astype(f32)).astype(bf16)
    sums = [[summed[n, dz] for dz in range(2)] for n in range(2)]
    place, *flat = lax.optimization_barrier((place, *sums[0], *sums[1]))
    sums[:2] = [flat[:2], flat[2:]]
    place, kept, given = call(place, pieces(2, mark) + [first, second], coulombs[2], matrices)
    sums.append(core_sum(kept[0], given[0], (True, True)))
    place, *sums[2] = lax.optimization_barrier((place, *sums[2]))
    place, kept, given = call(place, pieces(3, mark) + [first, second], coulombs[2], matrices)
    crossed = receive(given[0, 1], sibling)
    crossed_0 = receive(given[0, 0], sibling)
    leaving = (kept[0, 1].astype(f32) + crossed.astype(f32)).astype(bf16)
    leaving, kept_0 = lax.optimization_barrier((leaving, kept[0, 0]))
    sums.append([kept_0.astype(f32) + crossed_0.astype(f32), leaving])
    arrived = {}
    for n, ((dy, dx), both) in enumerate(zip(orders, sums)):
        for dz in range(2):
            if (dy, dx, dz) != (0, 0, 0):
                arrived[n, dz] = receive(both[dz], offset_source(dy, dx, dz, 0)).astype(f32)
    early = sum((arrived[n, dz] for n in range(3) for dz in range(2)), sums[3][0])
    early = lax.optimization_barrier(early)
    return -(early + arrived[3, 1])[None]


def solution(mesh):
    in_specs = (P("tgt", "grp", None, None), P("tgt", None, None, None), P(), P(), P())
    out_specs = P("tgt", "grp", None, None)

    return jax.shard_map(body, mesh=mesh, in_specs=in_specs, out_specs=out_specs, check_vma=False)
```

```python
import functools
import math

import jax
import jax.numpy as jnp
import numpy as np
from jax import lax
from jax.experimental import pallas as pl
from jax.experimental.pallas import tpu as pltpu
from jax.sharding import PartitionSpec as P


coulomb_scale = 0.1
points = 64
lanes = 2 * points
quarter = 16
splits = 4
pitch = 72
axes = ("tgt", "grp")
f32 = jnp.float32
bf16 = jnp.bfloat16


devices = [
    (zh, y, x, zl, c)
    for zh in range(2)
    for y in range(4)
    for x in range(4)
    for zl in range(2)
    for c in range(2)
]
number = {device: i for i, device in enumerate(devices)}


def outer(i):
    return (i + 3) % 4 if i % 2 == 0 else (i + 1) % 4


def first_source(zh, y, x, zl, c):
    return {
        (0, 0): (zh, y, outer(x), 0, 0),
        (0, 1): (zh ^ 1, outer(y), x, 1, 0),
        (1, 0): (zh, y, x, 1, 1),
        (1, 1): (zh ^ 1, outer(y), outer(x), 0, 1),
    }[zl, c]


def second_source(zh, y, x, zl, c):
    return {
        (0, 0): (zh, outer(y), outer(x), 0, 0),
        (0, 1): (zh ^ 1, y, x, 1, 0),
        (1, 0): (zh, outer(y), x, 1, 1),
        (1, 1): (zh ^ 1, y, outer(x), 0, 1),
    }[zl, c]


def offset_source(dy, dx, dz, dc):
    return lambda zh, y, x, zl, c: (zh, y ^ dy, x ^ dx, zl ^ dz, c ^ dc)


def receive(value, source):
    pairs = [(number[source(*device)], number[device]) for device in devices]
    return lax.ppermute(value, axes, pairs)


def slot_table():
    slot = lambda d: (d[0] * 4 + d[1]) * 4 + d[2]
    return np.array(
        [[slot(first_source(*d)), slot(second_source(*d))] for d in devices], np.int32
    )


def tables():
    indices = np.arange(points)
    phases = indices[:, None] * indices[None, :] % points
    angles = phases.astype(np.float32) * np.float32(2.0 * math.pi / points)
    scale = np.float32(1.0 / math.sqrt(points))
    rounded = lambda t: (t * scale).astype(bf16).astype(np.float32)
    return rounded(np.cos(angles)), rounded(np.sin(angles))


def section_matrices():
    cosine, sine = tables()
    both = lambda t: np.kron(np.eye(2, dtype=np.float32), t)
    left_forward = np.block([[cosine, sine], [-sine, cosine]])
    left_inverse = np.block([[cosine, -sine], [sine, cosine]])
    right_forward = np.block([[both(cosine), both(-sine)], [both(sine), both(cosine)]])
    right_inverse = np.block([[both(cosine), both(sine)], [both(-sine), both(cosine)]])
    return [
        jnp.asarray(m, bf16) for m in (left_forward, left_inverse, right_forward, right_inverse)
    ]


def pair_weights(occupations, slot_partner, slots):
    ids = jnp.arange(occupations.shape[0], dtype=jnp.int32)
    match = slot_partner[:, None] == ids[None, :]
    by_slot = jnp.sum(jnp.where(match, occupations[None, :], 0.0), axis=1)
    return jnp.sum(jnp.where(slots[:, None] == ids[None, :], by_slot[None, :], 0.0), axis=1)


def coulomb_kernel(screening, weights):
    indices = jnp.arange(points, dtype=jnp.int32)
    signed = jnp.where(indices < points // 2, indices, indices - points).astype(f32) * (
        2.0 * math.pi / points
    )
    squares = signed * signed
    wave_sq = squares[:, None, None] + squares[None, :, None] + jnp.tile(squares, 2)[None, None, :]
    screen_wave = screening[0] * (2.0 * math.pi / points)
    lane = jnp.arange(lanes, dtype=jnp.int32)
    weight = jnp.where(lane < points, weights[0], weights[1])
    return (coulomb_scale / (wave_sq + screen_wave * screen_wave)) * weight[None, None, :]


def pair_kernel(two_targets, stage, *refs):
    refs = list(refs)
    take = lambda count: [refs.pop(0) for _ in range(count)]
    (place_ref,) = take(1)
    if two_targets:
        targets = [take(4), take(4)]
        (shared,) = take(1)
    else:
        shared = take(4)
        partners = take(2)
    coulomb, lf_ref, li_ref, rf_ref, ri_ref = take(5)
    earlier = take(2) if stage == "last" else []
    outs = take(2)
    results_count = 2 if two_targets else 1
    x_v, a_v, b_v, k_v, s_ref, z_ref, y_ref, o_v, e_v, in_sem, k_sem, e_sem, out_sem = refs

    dot = functools.partial(jnp.dot, preferred_element_type=f32)
    place = place_ref[0]
    rows = quarter * points
    low = lax.broadcasted_iota(jnp.int16, (rows, lanes), 1) < points

    def block_of(step):
        return place ^ step

    def fetches(step, n):
        planes = pl.ds(block_of(step) * quarter, quarter)
        if two_targets:
            sources = [shared.at[planes], targets[0][n], targets[1][n]]
        else:
            sources = [shared[n], partners[0].at[planes], partners[1].at[planes]]
        return [
            pltpu.make_async_copy(source, v.at[step], in_sem.at[step, i])
            for i, (source, v) in enumerate(zip(sources, (x_v, a_v, b_v)))
        ]

    for step in range(4):
        for copy in fetches(step, step):
            copy.start()
    k_copy = pltpu.make_async_copy(coulomb, k_v, k_sem)
    k_copy.start()
    e_copies = [
        pltpu.make_async_copy(source, e_v.at[dc], e_sem.at[dc]) for dc, source in enumerate(earlier)
    ]
    for copy in e_copies:
        copy.start()
    lf = lf_ref[...]
    li = li_ref[...]

    def load(ref, step):
        return ref[step].reshape(rows, lanes)

    def swap(v):
        return pltpu.roll(v, points, 1)

    def planes_of(v):
        return v.reshape(quarter, points, lanes)

    def last_section(field, matrix):
        part = rows // splits
        parts = [dot(field[n * part : (n + 1) * part], matrix).astype(bf16) for n in range(splits)]
        return jnp.concatenate(parts, axis=0)

    def arrive(step):
        for copy in fetches(step, 0):
            copy.wait()

    def forward_z(step):
        x = load(x_v, step)
        swapped = swap(x)
        x_real = jnp.where(low, x, swapped)
        x_imag = jnp.where(low, swapped, x)
        a = load(a_v, step)
        b = load(b_v, step)
        q_real = jnp.where(low, a, swap(b))
        q_imag = jnp.where(low, swap(a), b)
        p_real, p_imag = (x_real, x_imag) if two_targets else (q_real, q_imag)
        t_real, t_imag = (q_real, q_imag) if two_targets else (x_real, x_imag)
        a_v[step] = planes_of(p_real)
        b_v[step] = planes_of(p_imag)
        density = jnp.concatenate(
            [p_real * t_real + p_imag * t_imag, p_real * t_imag - p_imag * t_real], axis=1
        )
        along_z = last_section(density, rf_ref[...])
        slot = step % 2
        for j in range(quarter):
            for c in range(2):
                z_ref[slot, j, c * points : (c + 1) * points] = along_z[
                    j * points : (j + 1) * points, c * lanes : (c + 1) * lanes
                ]

    def forward_y(step):
        slot = step % 2
        plane = block_of(step) * quarter
        along_y = dot(lf, jnp.concatenate([z_ref[slot, j] for j in range(quarter)], axis=1))
        for j in range(quarter):
            s_ref[pl.ds(plane + j, lanes, stride=pitch), :] = along_y[:, j * lanes : (j + 1) * lanes]

    arrive(0)
    forward_z(0)
    for step in range(3):
        arrive(step + 1)
    for step in range(3):
        forward_y(step)
        forward_z(step + 1)
    forward_y(3)
    k_copy.wait()

    def line(k, part):
        return pl.ds(pl.multiple_of((part * points + k) * pitch, 8), points)

    def middle(i, carry):
        first = i * quarter
        columns = []
        for j in range(quarter):
            parts = [s_ref[line(first + j, part), :].astype(bf16) for part in range(2)]
            columns.append(jnp.concatenate(parts, axis=0))
        spectrum = dot(lf, jnp.concatenate(columns, axis=1))
        weights = jnp.concatenate([k_v[first + j] for j in range(quarter)], axis=1)
        scaled = (spectrum * jnp.concatenate([weights, weights], axis=0)).astype(bf16)
        along_x = dot(li, scaled)
        for j in range(quarter):
            for part in range(2):
                s_ref[line(first + j, part), :] = along_x[
                    part * points : (part + 1) * points, j * lanes : (j + 1) * lanes
                ]
        return carry

    lax.fori_loop(0, 4, middle, 0)
    for copy in e_copies:
        copy.wait()

    def put(step, dc):
        return [
            pltpu.make_async_copy(
                o_v.at[i, step], outs[dc].at[i, step // 2], out_sem.at[i, step]
            )
            for i in range(results_count)
        ]

    def inverse_y(step):
        slot = step % 2
        plane = block_of(step) * quarter
        columns = [
            s_ref[pl.ds(plane + j, lanes, stride=pitch), :].astype(bf16) for j in range(quarter)
        ]
        along_y = dot(li, jnp.concatenate(columns, axis=1)).astype(bf16)
        for j in range(quarter):
            for c in range(2):
                y_ref[slot, j * points : (j + 1) * points, c * lanes : (c + 1) * lanes] = along_y[
                    c * points : (c + 1) * points, j * lanes : (j + 1) * lanes
                ]

    def inverse_z(step):
        potential = last_section(y_ref[step % 2], ri_ref[...])
        v_real = potential[:, :lanes]
        v_imag = potential[:, lanes:]
        p_real = load(a_v, step)
        p_imag = load(b_v, step)
        real = v_real * p_real - v_imag * p_imag
        imag = v_real * p_imag + v_imag * p_real
        if stage == "first":
            results = [real, imag]
        elif stage == "last":
            real = real + e_v[step % 2, 0, step // 2].reshape(rows, lanes)
            imag = imag + e_v[step % 2, 1, step // 2].reshape(rows, lanes)
            results = [jnp.where(low, real, swap(imag)), jnp.where(low, swap(real), imag)]
        else:
            results = [jnp.where(low, real, imag) + swap(jnp.where(low, imag, real))]
        for i, result in enumerate(results):
            o_v[i, step] = planes_of(result)

    def inverse(step, carry):
        inverse_z(step)
        inverse_y(step + 1)
        for dc in range(2):

            @pl.when(step % 2 == dc)
            def _():
                for copy in put(step, dc):
                    copy.start()

        return carry

    inverse_y(0)
    if stage == "last":
        lax.fori_loop(0, 3, inverse, 0)
    else:
        for step in range(3):
            inverse_z(step)
            inverse_y(step + 1)
    inverse_z(3)
    for step in range(3 if stage == "last" else 0, 4):
        for copy in put(step, step % 2):
            copy.start()
    for step in range(4):
        for copy in put(step, step % 2):
            copy.wait()


def exchange_part(place, sides, coulomb, matrices, two_targets=False, stage="only", earlier=()):
    anywhere = pl.BlockSpec(memory_space=pl.ANY)
    scalar = pl.BlockSpec(memory_space=pltpu.SMEM)
    near = pl.BlockSpec(memory_space=pltpu.VMEM)
    planes = (4, quarter, points, lanes)
    results = 2 if two_targets else 1
    halves = (results, 2, quarter, points, lanes)
    return pl.pallas_call(
        functools.partial(pair_kernel, two_targets, stage),
        out_shape=[jax.ShapeDtypeStruct(halves, bf16)] * 2,
        in_specs=[scalar]
        + [anywhere] * (len(sides) + 1)
        + [near] * 4
        + [anywhere] * len(earlier),
        out_specs=[anywhere] * 2,
        scratch_shapes=[
            pltpu.VMEM(planes, bf16),
            pltpu.VMEM(planes, bf16),
            pltpu.VMEM(planes, bf16),
            pltpu.VMEM((points, points, lanes), f32),
            pltpu.VMEM((2 * points * pitch, lanes), f32),
            pltpu.VMEM((2, quarter, lanes, lanes), bf16),
            pltpu.VMEM((2, quarter * points, 2 * lanes), bf16),
            pltpu.VMEM((results, *planes), bf16),
            pltpu.VMEM((2, *halves), bf16),
            pltpu.SemaphoreType.DMA((4, 3)),
            pltpu.SemaphoreType.DMA,
            pltpu.SemaphoreType.DMA((2,)),
            pltpu.SemaphoreType.DMA((2, 4)),
        ],
        compiler_params=pltpu.CompilerParams(vmem_limit_bytes=40 << 20),
        cost_estimate=pl.CostEstimate(
            flops=5 * 10**9, bytes_accessed=24 * 2**20, transcendentals=0
        ),
    )(place, *sides, coulomb, *matrices, *earlier)


def body(targets, partners, occupations, slot_partner, screening):
    own = targets[0]
    partner = partners[0]
    first = receive(partner, first_source)
    orders = [(0, 1), (1, 0), (1, 1), (0, 0)]
    halves = []
    sent = own
    for n, (dy, dx) in enumerate(orders):
        if n == 2:
            sent, *halves[1] = lax.optimization_barrier((own, *halves[1]))
        half = []
        for dz in range(2):
            source = offset_source(dy, dx, dz, 0)
            half.append(own if (dy, dx) == (0, 0) else receive(sent, source))
        halves.append(half)
    matrices = section_matrices()
    device = lax.axis_index("tgt") * 4 + lax.axis_index("grp")
    slots = lax.dynamic_slice_in_dim(jnp.asarray(slot_table()), device, 1)[0]
    place = lax.axis_index("grp")[None].astype(jnp.int32)
    weights = pair_weights(occupations, slot_partner, slots)
    sibling = offset_source(0, 0, 0, 1)

    def pieces(n, mark=None):
        same, other = halves[n]
        if mark is not None:
            _, same, other = lax.optimization_barrier((mark, same, other))
        crossed = []
        for piece in (same, other):
            crossed.append(receive(piece, sibling))
        return [same, crossed[0], other, crossed[1]]

    def core_sum(kept, given, rounded):
        both = []
        for dz in range(2):
            crossed = receive(given[dz], sibling)
            summed = kept[dz].astype(f32) + crossed.astype(f32)
            both.append(summed.astype(bf16) if rounded[dz] else summed)
        return both

    def call(place, *args, **kwargs):
        parts = exchange_part(place, *args, **kwargs)
        return lax.optimization_barrier((place, *parts))

    coulombs = [
        coulomb_kernel(screening, (weights[a], weights[b])) for a, b in ((0, 0), (1, 1), (0, 1))
    ]
    coulombs[2], late = lax.optimization_barrier((coulombs[2], partner))
    second = receive(late, second_source)
    two = pieces(0) + pieces(1)
    place, *earlier = call(
        place, two + [first], coulombs[0], matrices, two_targets=True, stage="first"
    )
    mark = place
    place, kept, given = call(place, two + [second], coulombs[1], matrices, True, "last", earlier)
    crossed = receive(given, sibling)
    _, sent = lax.optimization_barrier((place, own))
    halves[3][1] = receive(sent, offset_source(0, 0, 1, 0))
    summed = (kept.astype(f32) + crossed.astype(f32)).astype(bf16)
    sums = [[summed[n, dz] for dz in range(2)] for n in range(2)]
    place, *flat = lax.optimization_barrier((place, *sums[0], *sums[1]))
    sums[:2] = [flat[:2], flat[2:]]
    place, kept, given = call(place, pieces(2, mark) + [first, second], coulombs[2], matrices)
    sums.append(core_sum(kept[0], given[0], (True, True)))
    place, *sums[2] = lax.optimization_barrier((place, *sums[2]))
    place, kept, given = call(place, pieces(3, mark) + [first, second], coulombs[2], matrices)
    crossed = receive(given[0, 1], sibling)
    crossed_0 = receive(given[0, 0], sibling)
    leaving = (kept[0, 1].astype(f32) + crossed.astype(f32)).astype(bf16)
    leaving, kept_0 = lax.optimization_barrier((leaving, kept[0, 0]))
    sums.append([kept_0.astype(f32) + crossed_0.astype(f32), leaving])
    arrived = {}
    for n, ((dy, dx), both) in enumerate(zip(orders, sums)):
        for dz in range(2):
            if (dy, dx, dz) != (0, 0, 0):
                arrived[n, dz] = receive(both[dz], offset_source(dy, dx, dz, 0)).astype(f32)
    early = sum((arrived[n, dz] for n in range(3) for dz in range(2)), sums[3][0])
    early = lax.optimization_barrier(early)
    return -(early + arrived[3, 1])[None]


def solution(mesh):
    in_specs = (P("tgt", "grp", None, None), P("tgt", None, None, None), P(), P(), P())
    out_specs = P("tgt", "grp", None, None)

    return jax.shard_map(body, mesh=mesh, in_specs=in_specs, out_specs=out_specs, check_vma=False)
```

```python
import functools
import math

import jax
import jax.numpy as jnp
import numpy as np
from jax import lax
from jax.experimental import pallas as pl
from jax.experimental.pallas import tpu as pltpu
from jax.sharding import PartitionSpec as P


coulomb_scale = 0.1
points = 64
lanes = 2 * points
quarter = 16
splits = 4
pitch = 72
axes = ("tgt", "grp")
f32 = jnp.float32
bf16 = jnp.bfloat16


devices = [
    (zh, y, x, zl, c)
    for zh in range(2)
    for y in range(4)
    for x in range(4)
    for zl in range(2)
    for c in range(2)
]
number = {device: i for i, device in enumerate(devices)}


def outer(i):
    return (i + 3) % 4 if i % 2 == 0 else (i + 1) % 4


def first_source(zh, y, x, zl, c):
    return {
        (0, 0): (zh, y, outer(x), 0, 0),
        (0, 1): (zh ^ 1, outer(y), outer(x), 1, 0),
        (1, 0): (zh, y, x, 1, 1),
        (1, 1): (zh ^ 1, outer(y), x, 0, 1),
    }[zl, c]


def second_source(zh, y, x, zl, c):
    return {
        (0, 0): (zh, outer(y), outer(x), 0, 0),
        (0, 1): (zh ^ 1, y, outer(x), 1, 0),
        (1, 0): (zh, outer(y), x, 1, 1),
        (1, 1): (zh ^ 1, y, x, 0, 1),
    }[zl, c]


def offset_source(dy, dx, dz, dc):
    return lambda zh, y, x, zl, c: (zh, y ^ dy, x ^ dx, zl ^ dz, c ^ dc)


def receive(value, source):
    pairs = [(number[source(*device)], number[device]) for device in devices]
    return lax.ppermute(value, axes, pairs)


def slot_table():
    slot = lambda d: (d[0] * 4 + d[1]) * 4 + d[2]
    return np.array(
        [[slot(first_source(*d)), slot(second_source(*d))] for d in devices], np.int32
    )


def tables():
    indices = np.arange(points)
    phases = indices[:, None] * indices[None, :] % points
    angles = phases.astype(np.float32) * np.float32(2.0 * math.pi / points)
    scale = np.float32(1.0 / math.sqrt(points))
    rounded = lambda t: (t * scale).astype(bf16).astype(np.float32)
    return rounded(np.cos(angles)), rounded(np.sin(angles))


def section_matrices():
    cosine, sine = tables()
    both = lambda t: np.kron(np.eye(2, dtype=np.float32), t)
    left_forward = np.block([[cosine, sine], [-sine, cosine]])
    left_inverse = np.block([[cosine, -sine], [sine, cosine]])
    right_forward = np.block([[both(cosine), both(-sine)], [both(sine), both(cosine)]])
    right_inverse = np.block([[both(cosine), both(sine)], [both(-sine), both(cosine)]])
    return [
        jnp.asarray(m, bf16) for m in (left_forward, left_inverse, right_forward, right_inverse)
    ]


def pair_weights(occupations, slot_partner, slots):
    ids = jnp.arange(occupations.shape[0], dtype=jnp.int32)
    match = slot_partner[:, None] == ids[None, :]
    by_slot = jnp.sum(jnp.where(match, occupations[None, :], 0.0), axis=1)
    return jnp.sum(jnp.where(slots[:, None] == ids[None, :], by_slot[None, :], 0.0), axis=1)


def coulomb_kernel(screening, weights):
    indices = jnp.arange(points, dtype=jnp.int32)
    signed = jnp.where(indices < points // 2, indices, indices - points).astype(f32) * (
        2.0 * math.pi / points
    )
    squares = signed * signed
    wave_sq = squares[:, None, None] + squares[None, :, None] + jnp.tile(squares, 2)[None, None, :]
    screen_wave = screening[0] * (2.0 * math.pi / points)
    lane = jnp.arange(lanes, dtype=jnp.int32)
    weight = jnp.where(lane < points, weights[0], weights[1])
    return (coulomb_scale / (wave_sq + screen_wave * screen_wave)) * weight[None, None, :]


def pair_kernel(two_targets, stage, *refs):
    refs = list(refs)
    take = lambda count: [refs.pop(0) for _ in range(count)]
    (place_ref,) = take(1)
    if two_targets:
        targets = [take(4), take(4)]
        (shared,) = take(1)
    else:
        shared = take(4)
        partners = take(2)
    coulomb, lf_ref, li_ref, rf_ref, ri_ref = take(5)
    earlier = take(2) if stage == "last" else []
    outs = take(2)
    results_count = 2 if two_targets else 1
    x_v, a_v, b_v, k_v, s_ref, z_ref, y_ref, o_v, e_v, in_sem, k_sem, e_sem, out_sem = refs

    dot = functools.partial(jnp.dot, preferred_element_type=f32)
    place = place_ref[0]
    rows = quarter * points
    low = lax.broadcasted_iota(jnp.int16, (rows, lanes), 1) < points

    def block_of(step):
        return place ^ step

    def fetches(step, n):
        planes = pl.ds(block_of(step) * quarter, quarter)
        if two_targets:
            sources = [shared.at[planes], targets[0][n], targets[1][n]]
        else:
            sources = [shared[n], partners[0].at[planes], partners[1].at[planes]]
        return [
            pltpu.make_async_copy(source, v.at[step], in_sem.at[step, i])
            for i, (source, v) in enumerate(zip(sources, (x_v, a_v, b_v)))
        ]

    for step in range(4):
        for copy in fetches(step, step):
            copy.start()
    k_copy = pltpu.make_async_copy(coulomb, k_v, k_sem)
    k_copy.start()
    e_copies = [
        pltpu.make_async_copy(source, e_v.at[dc], e_sem.at[dc]) for dc, source in enumerate(earlier)
    ]
    for copy in e_copies:
        copy.start()
    lf = lf_ref[...]
    li = li_ref[...]

    def load(ref, step):
        return ref[step].reshape(rows, lanes)

    def swap(v):
        return pltpu.roll(v, points, 1)

    def planes_of(v):
        return v.reshape(quarter, points, lanes)

    def last_section(field, matrix):
        part = rows // splits
        parts = [dot(field[n * part : (n + 1) * part], matrix).astype(bf16) for n in range(splits)]
        return jnp.concatenate(parts, axis=0)

    def arrive(step):
        for copy in fetches(step, 0):
            copy.wait()

    def forward_z(step):
        x = load(x_v, step)
        swapped = swap(x)
        x_real = jnp.where(low, x, swapped)
        x_imag = jnp.where(low, swapped, x)
        a = load(a_v, step)
        b = load(b_v, step)
        q_real = jnp.where(low, a, swap(b))
        q_imag = jnp.where(low, swap(a), b)
        p_real, p_imag = (x_real, x_imag) if two_targets else (q_real, q_imag)
        t_real, t_imag = (q_real, q_imag) if two_targets else (x_real, x_imag)
        a_v[step] = planes_of(p_real)
        b_v[step] = planes_of(p_imag)
        density = jnp.concatenate(
            [p_real * t_real + p_imag * t_imag, p_real * t_imag - p_imag * t_real], axis=1
        )
        along_z = last_section(density, rf_ref[...])
        slot = step % 2
        for j in range(quarter):
            for c in range(2):
                z_ref[slot, j, c * points : (c + 1) * points] = along_z[
                    j * points : (j + 1) * points, c * lanes : (c + 1) * lanes
                ]

    def forward_y(step):
        slot = step % 2
        plane = block_of(step) * quarter
        along_y = dot(lf, jnp.concatenate([z_ref[slot, j] for j in range(quarter)], axis=1))
        for j in range(quarter):
            s_ref[pl.ds(plane + j, lanes, stride=pitch), :] = along_y[:, j * lanes : (j + 1) * lanes]

    arrive(0)
    forward_z(0)
    for step in range(3):
        arrive(step + 1)
    for step in range(3):
        forward_y(step)
        forward_z(step + 1)
    forward_y(3)
    k_copy.wait()

    def line(k, part):
        return pl.ds(pl.multiple_of((part * points + k) * pitch, 8), points)

    def middle(i, carry):
        first = i * quarter
        columns = []
        for j in range(quarter):
            parts = [s_ref[line(first + j, part), :].astype(bf16) for part in range(2)]
            columns.append(jnp.concatenate(parts, axis=0))
        spectrum = dot(lf, jnp.concatenate(columns, axis=1))
        weights = jnp.concatenate([k_v[first + j] for j in range(quarter)], axis=1)
        scaled = (spectrum * jnp.concatenate([weights, weights], axis=0)).astype(bf16)
        along_x = dot(li, scaled)
        for j in range(quarter):
            for part in range(2):
                s_ref[line(first + j, part), :] = along_x[
                    part * points : (part + 1) * points, j * lanes : (j + 1) * lanes
                ]
        return carry

    lax.fori_loop(0, 4, middle, 0)
    for copy in e_copies:
        copy.wait()

    def put(step, dc):
        return [
            pltpu.make_async_copy(
                o_v.at[i, step], outs[dc].at[i, step // 2], out_sem.at[i, step]
            )
            for i in range(results_count)
        ]

    def inverse_y(step):
        slot = step % 2
        plane = block_of(step) * quarter
        columns = [
            s_ref[pl.ds(plane + j, lanes, stride=pitch), :].astype(bf16) for j in range(quarter)
        ]
        along_y = dot(li, jnp.concatenate(columns, axis=1)).astype(bf16)
        for j in range(quarter):
            for c in range(2):
                y_ref[slot, j * points : (j + 1) * points, c * lanes : (c + 1) * lanes] = along_y[
                    c * points : (c + 1) * points, j * lanes : (j + 1) * lanes
                ]

    def inverse_z(step):
        potential = last_section(y_ref[step % 2], ri_ref[...])
        v_real = potential[:, :lanes]
        v_imag = potential[:, lanes:]
        p_real = load(a_v, step)
        p_imag = load(b_v, step)
        real = v_real * p_real - v_imag * p_imag
        imag = v_real * p_imag + v_imag * p_real
        if stage == "first":
            results = [real, imag]
        elif stage == "last":
            real = real + e_v[step % 2, 0, step // 2].reshape(rows, lanes)
            imag = imag + e_v[step % 2, 1, step // 2].reshape(rows, lanes)
            results = [jnp.where(low, real, swap(imag)), jnp.where(low, swap(real), imag)]
        else:
            results = [jnp.where(low, real, imag) + swap(jnp.where(low, imag, real))]
        for i, result in enumerate(results):
            o_v[i, step] = planes_of(result)

    def inverse(step, carry):
        inverse_z(step)
        inverse_y(step + 1)
        for dc in range(2):

            @pl.when(step % 2 == dc)
            def _():
                for copy in put(step, dc):
                    copy.start()

        return carry

    inverse_y(0)
    if stage == "last":
        lax.fori_loop(0, 3, inverse, 0)
    else:
        for step in range(3):
            inverse_z(step)
            inverse_y(step + 1)
    inverse_z(3)
    for step in range(3 if stage == "last" else 0, 4):
        for copy in put(step, step % 2):
            copy.start()
    for step in range(4):
        for copy in put(step, step % 2):
            copy.wait()


def exchange_part(place, sides, coulomb, matrices, two_targets=False, stage="only", earlier=()):
    anywhere = pl.BlockSpec(memory_space=pl.ANY)
    scalar = pl.BlockSpec(memory_space=pltpu.SMEM)
    near = pl.BlockSpec(memory_space=pltpu.VMEM)
    planes = (4, quarter, points, lanes)
    results = 2 if two_targets else 1
    halves = (results, 2, quarter, points, lanes)
    return pl.pallas_call(
        functools.partial(pair_kernel, two_targets, stage),
        out_shape=[jax.ShapeDtypeStruct(halves, bf16)] * 2,
        in_specs=[scalar]
        + [anywhere] * (len(sides) + 1)
        + [near] * 4
        + [anywhere] * len(earlier),
        out_specs=[anywhere] * 2,
        scratch_shapes=[
            pltpu.VMEM(planes, bf16),
            pltpu.VMEM(planes, bf16),
            pltpu.VMEM(planes, bf16),
            pltpu.VMEM((points, points, lanes), f32),
            pltpu.VMEM((2 * points * pitch, lanes), f32),
            pltpu.VMEM((2, quarter, lanes, lanes), bf16),
            pltpu.VMEM((2, quarter * points, 2 * lanes), bf16),
            pltpu.VMEM((results, *planes), bf16),
            pltpu.VMEM((2, *halves), bf16),
            pltpu.SemaphoreType.DMA((4, 3)),
            pltpu.SemaphoreType.DMA,
            pltpu.SemaphoreType.DMA((2,)),
            pltpu.SemaphoreType.DMA((2, 4)),
        ],
        compiler_params=pltpu.CompilerParams(vmem_limit_bytes=40 << 20),
        cost_estimate=pl.CostEstimate(
            flops=5 * 10**9, bytes_accessed=24 * 2**20, transcendentals=0
        ),
    )(place, *sides, coulomb, *matrices, *earlier)


def body(targets, partners, occupations, slot_partner, screening):
    own = targets[0]
    partner = partners[0]
    first = receive(partner, first_source)
    orders = [(0, 1), (1, 0), (1, 1), (0, 0)]
    halves = []
    sent = own
    for n, (dy, dx) in enumerate(orders):
        if n == 2:
            sent, *halves[1] = lax.optimization_barrier((own, *halves[1]))
        half = []
        for dz in range(2):
            source = offset_source(dy, dx, dz, 0)
            half.append(own if (dy, dx, dz) == (0, 0, 0) else receive(sent, source))
        halves.append(half)
    matrices = section_matrices()
    device = lax.axis_index("tgt") * 4 + lax.axis_index("grp")
    slots = lax.dynamic_slice_in_dim(jnp.asarray(slot_table()), device, 1)[0]
    place = lax.axis_index("grp")[None].astype(jnp.int32)
    weights = pair_weights(occupations, slot_partner, slots)
    sibling = offset_source(0, 0, 0, 1)

    def pieces(n, mark=None):
        same, other = halves[n]
        if mark is not None:
            _, same, other = lax.optimization_barrier((mark, same, other))
        crossed = []
        for piece in (same, other):
            crossed.append(receive(piece, sibling))
        return [same, crossed[0], other, crossed[1]]

    def core_sum(kept, given, rounded):
        both = []
        for dz in range(2):
            crossed = receive(given[dz], sibling)
            summed = kept[dz].astype(f32) + crossed.astype(f32)
            both.append(summed.astype(bf16) if rounded[dz] else summed)
        return both

    def call(place, *args, **kwargs):
        parts = exchange_part(place, *args, **kwargs)
        return lax.optimization_barrier((place, *parts))

    coulombs = [
        coulomb_kernel(screening, (weights[a], weights[b])) for a, b in ((0, 0), (1, 1), (0, 1))
    ]
    coulombs[2], late = lax.optimization_barrier((coulombs[2], partner))
    second = receive(late, second_source)
    two = pieces(0) + pieces(1)
    place, *earlier = call(
        place, two + [first], coulombs[0], matrices, two_targets=True, stage="first"
    )
    mark = place
    place, kept, given = call(place, two + [second], coulombs[1], matrices, True, "last", earlier)
    crossed = receive(given, sibling)
    summed = (kept.astype(f32) + crossed.astype(f32)).astype(bf16)
    sums = [[summed[n, dz] for dz in range(2)] for n in range(2)]
    place, *flat = lax.optimization_barrier((place, *sums[0], *sums[1]))
    sums[:2] = [flat[:2], flat[2:]]
    place, kept, given = call(place, pieces(2, mark) + [first, second], coulombs[2], matrices)
    sums.append(core_sum(kept[0], given[0], (True, True)))
    place, *sums[2] = lax.optimization_barrier((place, *sums[2]))
    place, kept, given = call(place, pieces(3, mark) + [first, second], coulombs[2], matrices)
    crossed = receive(given[0, 1], sibling)
    crossed_0 = receive(given[0, 0], sibling)
    leaving = (kept[0, 1].astype(f32) + crossed.astype(f32)).astype(bf16)
    leaving, kept_0 = lax.optimization_barrier((leaving, kept[0, 0]))
    sums.append([kept_0.astype(f32) + crossed_0.astype(f32), leaving])
    arrived = {}
    for n, ((dy, dx), both) in enumerate(zip(orders, sums)):
        for dz in range(2):
            if (dy, dx, dz) != (0, 0, 0):
                arrived[n, dz] = receive(both[dz], offset_source(dy, dx, dz, 0)).astype(f32)
    early = sum((arrived[n, dz] for n in range(3) for dz in range(2)), sums[3][0])
    early = lax.optimization_barrier(early)
    return -(early + arrived[3, 1])[None]


def solution(mesh):
    in_specs = (P("tgt", "grp", None, None), P("tgt", None, None, None), P(), P(), P())
    out_specs = P("tgt", "grp", None, None)

    return jax.shard_map(body, mesh=mesh, in_specs=in_specs, out_specs=out_specs, check_vma=False)
```

```python
import functools
import math

import jax
import jax.numpy as jnp
import numpy as np
from jax import lax
from jax.experimental import pallas as pl
from jax.experimental.pallas import tpu as pltpu
from jax.sharding import PartitionSpec as P


coulomb_scale = 0.1
points = 64
lanes = 2 * points
quarter = 16
splits = 4
pitch = 72
axes = ("tgt", "grp")
f32 = jnp.float32
bf16 = jnp.bfloat16


devices = [
    (zh, y, x, zl, c)
    for zh in range(2)
    for y in range(4)
    for x in range(4)
    for zl in range(2)
    for c in range(2)
]
number = {device: i for i, device in enumerate(devices)}


def outer(i):
    return (i + 3) % 4 if i % 2 == 0 else (i + 1) % 4


def first_source(zh, y, x, zl, c):
    return {
        (0, 0): (zh, y, x, 0, 1),
        (0, 1): (zh ^ 1, y, x, 1, 0),
        (1, 0): (zh, outer(y), x, 1, 1),
        (1, 1): (zh ^ 1, y, outer(x), 0, 0),
    }[zl, c]


def second_source(zh, y, x, zl, c):
    return {
        (0, 0): (zh, outer(y), outer(x), 0, 1),
        (0, 1): (zh ^ 1, outer(y), outer(x), 1, 0),
        (1, 0): (zh, y, outer(x), 1, 1),
        (1, 1): (zh ^ 1, outer(y), x, 0, 0),
    }[zl, c]


def offset_source(dy, dx, dz, dc):
    return lambda zh, y, x, zl, c: (zh, y ^ dy, x ^ dx, zl ^ dz, c ^ dc)


def receive(value, source):
    pairs = [(number[source(*device)], number[device]) for device in devices]
    return lax.ppermute(value, axes, pairs)


def slot_table():
    slot = lambda d: (d[0] * 4 + d[1]) * 4 + d[2]
    return np.array(
        [[slot(first_source(*d)), slot(second_source(*d))] for d in devices], np.int32
    )


def tables():
    indices = np.arange(points)
    phases = indices[:, None] * indices[None, :] % points
    angles = phases.astype(np.float32) * np.float32(2.0 * math.pi / points)
    scale = np.float32(1.0 / math.sqrt(points))
    rounded = lambda t: (t * scale).astype(bf16).astype(np.float32)
    return rounded(np.cos(angles)), rounded(np.sin(angles))


def section_matrices():
    cosine, sine = tables()
    both = lambda t: np.kron(np.eye(2, dtype=np.float32), t)
    left_forward = np.block([[cosine, sine], [-sine, cosine]])
    left_inverse = np.block([[cosine, -sine], [sine, cosine]])
    right_forward = np.block([[both(cosine), both(-sine)], [both(sine), both(cosine)]])
    right_inverse = np.block([[both(cosine), both(sine)], [both(-sine), both(cosine)]])
    return [
        jnp.asarray(m, bf16) for m in (left_forward, left_inverse, right_forward, right_inverse)
    ]


def pair_weights(occupations, slot_partner, slots):
    ids = jnp.arange(occupations.shape[0], dtype=jnp.int32)
    match = slot_partner[:, None] == ids[None, :]
    by_slot = jnp.sum(jnp.where(match, occupations[None, :], 0.0), axis=1)
    return jnp.sum(jnp.where(slots[:, None] == ids[None, :], by_slot[None, :], 0.0), axis=1)


def coulomb_kernel(screening, weights):
    indices = jnp.arange(points, dtype=jnp.int32)
    signed = jnp.where(indices < points // 2, indices, indices - points).astype(f32) * (
        2.0 * math.pi / points
    )
    squares = signed * signed
    wave_sq = squares[:, None, None] + squares[None, :, None] + jnp.tile(squares, 2)[None, None, :]
    screen_wave = screening[0] * (2.0 * math.pi / points)
    lane = jnp.arange(lanes, dtype=jnp.int32)
    weight = jnp.where(lane < points, weights[0], weights[1])
    return (coulomb_scale / (wave_sq + screen_wave * screen_wave)) * weight[None, None, :]


def pair_kernel(two_targets, stage, *refs):
    refs = list(refs)
    take = lambda count: [refs.pop(0) for _ in range(count)]
    (place_ref,) = take(1)
    if two_targets:
        targets = [take(4), take(4)]
        (shared,) = take(1)
    else:
        shared = take(4)
        partners = take(2)
    coulomb, lf_ref, li_ref, rf_ref, ri_ref = take(5)
    earlier = take(2) if stage == "last" else []
    outs = take(2)
    results_count = 2 if two_targets else 1
    x_v, a_v, b_v, k_v, s_ref, z_ref, y_ref, o_v, e_v, in_sem, k_sem, e_sem, out_sem = refs

    dot = functools.partial(jnp.dot, preferred_element_type=f32)
    place = place_ref[0]
    rows = quarter * points
    low = lax.broadcasted_iota(jnp.int16, (rows, lanes), 1) < points

    def block_of(step):
        return place ^ step

    def fetches(step, n):
        planes = pl.ds(block_of(step) * quarter, quarter)
        if two_targets:
            sources = [shared.at[planes], targets[0][n], targets[1][n]]
        else:
            sources = [shared[n], partners[0].at[planes], partners[1].at[planes]]
        return [
            pltpu.make_async_copy(source, v.at[step], in_sem.at[step, i])
            for i, (source, v) in enumerate(zip(sources, (x_v, a_v, b_v)))
        ]

    for step in range(4):
        for copy in fetches(step, step):
            copy.start()
    k_copy = pltpu.make_async_copy(coulomb, k_v, k_sem)
    k_copy.start()
    e_copies = [
        pltpu.make_async_copy(source, e_v.at[dc], e_sem.at[dc]) for dc, source in enumerate(earlier)
    ]
    for copy in e_copies:
        copy.start()
    lf = lf_ref[...]
    li = li_ref[...]

    def load(ref, step):
        return ref[step].reshape(rows, lanes)

    def swap(v):
        return pltpu.roll(v, points, 1)

    def planes_of(v):
        return v.reshape(quarter, points, lanes)

    def last_section(field, matrix):
        part = rows // splits
        parts = [dot(field[n * part : (n + 1) * part], matrix).astype(bf16) for n in range(splits)]
        return jnp.concatenate(parts, axis=0)

    def arrive(step):
        for copy in fetches(step, 0):
            copy.wait()

    def forward_z(step):
        x = load(x_v, step)
        swapped = swap(x)
        x_real = jnp.where(low, x, swapped)
        x_imag = jnp.where(low, swapped, x)
        a = load(a_v, step)
        b = load(b_v, step)
        q_real = jnp.where(low, a, swap(b))
        q_imag = jnp.where(low, swap(a), b)
        p_real, p_imag = (x_real, x_imag) if two_targets else (q_real, q_imag)
        t_real, t_imag = (q_real, q_imag) if two_targets else (x_real, x_imag)
        a_v[step] = planes_of(p_real)
        b_v[step] = planes_of(p_imag)
        density = jnp.concatenate(
            [p_real * t_real + p_imag * t_imag, p_real * t_imag - p_imag * t_real], axis=1
        )
        along_z = last_section(density, rf_ref[...])
        slot = step % 2
        for j in range(quarter):
            for c in range(2):
                z_ref[slot, j, c * points : (c + 1) * points] = along_z[
                    j * points : (j + 1) * points, c * lanes : (c + 1) * lanes
                ]

    def forward_y(step):
        slot = step % 2
        plane = block_of(step) * quarter
        along_y = dot(lf, jnp.concatenate([z_ref[slot, j] for j in range(quarter)], axis=1))
        for j in range(quarter):
            s_ref[pl.ds(plane + j, lanes, stride=pitch), :] = along_y[:, j * lanes : (j + 1) * lanes]

    arrive(0)
    forward_z(0)
    for step in range(3):
        arrive(step + 1)
    for step in range(3):
        forward_y(step)
        forward_z(step + 1)
    forward_y(3)
    k_copy.wait()

    def line(k, part):
        return pl.ds(pl.multiple_of((part * points + k) * pitch, 8), points)

    def middle(i, carry):
        first = i * quarter
        columns = []
        for j in range(quarter):
            parts = [s_ref[line(first + j, part), :].astype(bf16) for part in range(2)]
            columns.append(jnp.concatenate(parts, axis=0))
        spectrum = dot(lf, jnp.concatenate(columns, axis=1))
        weights = jnp.concatenate([k_v[first + j] for j in range(quarter)], axis=1)
        scaled = (spectrum * jnp.concatenate([weights, weights], axis=0)).astype(bf16)
        along_x = dot(li, scaled)
        for j in range(quarter):
            for part in range(2):
                s_ref[line(first + j, part), :] = along_x[
                    part * points : (part + 1) * points, j * lanes : (j + 1) * lanes
                ]
        return carry

    lax.fori_loop(0, 4, middle, 0, unroll=2)
    for copy in e_copies:
        copy.wait()

    def put(step, dc):
        return [
            pltpu.make_async_copy(
                o_v.at[i, step], outs[dc].at[i, step // 2], out_sem.at[i, step]
            )
            for i in range(results_count)
        ]

    def inverse_y(step):
        slot = step % 2
        plane = block_of(step) * quarter
        columns = [
            s_ref[pl.ds(plane + j, lanes, stride=pitch), :].astype(bf16) for j in range(quarter)
        ]
        along_y = dot(li, jnp.concatenate(columns, axis=1)).astype(bf16)
        for j in range(quarter):
            for c in range(2):
                y_ref[slot, j * points : (j + 1) * points, c * lanes : (c + 1) * lanes] = along_y[
                    c * points : (c + 1) * points, j * lanes : (j + 1) * lanes
                ]

    def inverse_z(step):
        potential = last_section(y_ref[step % 2], ri_ref[...])
        v_real = potential[:, :lanes]
        v_imag = potential[:, lanes:]
        p_real = load(a_v, step)
        p_imag = load(b_v, step)
        real = v_real * p_real - v_imag * p_imag
        imag = v_real * p_imag + v_imag * p_real
        if stage == "first":
            results = [real, imag]
        elif stage == "last":
            real = real + e_v[step % 2, 0, step // 2].reshape(rows, lanes)
            imag = imag + e_v[step % 2, 1, step // 2].reshape(rows, lanes)
            results = [jnp.where(low, real, swap(imag)), jnp.where(low, swap(real), imag)]
        else:
            results = [jnp.where(low, real, imag) + swap(jnp.where(low, imag, real))]
        for i, result in enumerate(results):
            o_v[i, step] = planes_of(result)

    def inverse(step, carry):
        inverse_z(step)
        inverse_y(step + 1)
        for dc in range(2):

            @pl.when(step % 2 == dc)
            def _():
                for copy in put(step, dc):
                    copy.start()

        return carry

    inverse_y(0)
    if stage == "last":
        lax.fori_loop(0, 3, inverse, 0)
    else:
        for step in range(3):
            inverse_z(step)
            inverse_y(step + 1)
    inverse_z(3)
    for step in range(3 if stage == "last" else 0, 4):
        for copy in put(step, step % 2):
            copy.start()
    for step in range(4):
        for copy in put(step, step % 2):
            copy.wait()


def exchange_part(place, sides, coulomb, matrices, two_targets=False, stage="only", earlier=()):
    anywhere = pl.BlockSpec(memory_space=pl.ANY)
    scalar = pl.BlockSpec(memory_space=pltpu.SMEM)
    near = pl.BlockSpec(memory_space=pltpu.VMEM)
    planes = (4, quarter, points, lanes)
    results = 2 if two_targets else 1
    halves = (results, 2, quarter, points, lanes)
    return pl.pallas_call(
        functools.partial(pair_kernel, two_targets, stage),
        out_shape=[jax.ShapeDtypeStruct(halves, bf16)] * 2,
        in_specs=[scalar]
        + [anywhere] * (len(sides) + 1)
        + [near] * 4
        + [anywhere] * len(earlier),
        out_specs=[anywhere] * 2,
        scratch_shapes=[
            pltpu.VMEM(planes, bf16),
            pltpu.VMEM(planes, bf16),
            pltpu.VMEM(planes, bf16),
            pltpu.VMEM((points, points, lanes), f32),
            pltpu.VMEM((2 * points * pitch, lanes), f32),
            pltpu.VMEM((2, quarter, lanes, lanes), bf16),
            pltpu.VMEM((2, quarter * points, 2 * lanes), bf16),
            pltpu.VMEM((results, *planes), bf16),
            pltpu.VMEM((2, *halves), bf16),
            pltpu.SemaphoreType.DMA((4, 3)),
            pltpu.SemaphoreType.DMA,
            pltpu.SemaphoreType.DMA((2,)),
            pltpu.SemaphoreType.DMA((2, 4)),
        ],
        compiler_params=pltpu.CompilerParams(vmem_limit_bytes=40 << 20),
        cost_estimate=pl.CostEstimate(
            flops=5 * 10**9, bytes_accessed=24 * 2**20, transcendentals=0
        ),
    )(place, *sides, coulomb, *matrices, *earlier)


def body(targets, partners, occupations, slot_partner, screening):
    own = targets[0]
    partner = partners[0]
    first = receive(partner, first_source)
    orders = [(0, 1), (1, 0), (1, 1), (0, 0)]
    halves = []
    sent = own
    for n, (dy, dx) in enumerate(orders):
        if n == 2:
            sent, *halves[1] = lax.optimization_barrier((own, *halves[1]))
        half = []
        for dz in range(2):
            source = offset_source(dy, dx, dz, 0)
            half.append(own if (dy, dx) == (0, 0) else receive(sent, source))
        halves.append(half)
    second = receive(partner, second_source)
    matrices = section_matrices()
    device = lax.axis_index("tgt") * 4 + lax.axis_index("grp")
    slots = lax.dynamic_slice_in_dim(jnp.asarray(slot_table()), device, 1)[0]
    place = lax.axis_index("grp")[None].astype(jnp.int32)
    weights = pair_weights(occupations, slot_partner, slots)
    sibling = offset_source(0, 0, 0, 1)

    def pieces(n, mark=None):
        same, other = halves[n]
        if mark is not None:
            _, same, other = lax.optimization_barrier((mark, same, other))
        crossed = []
        for piece in (same, other):
            crossed.append(receive(piece, sibling))
        return [same, crossed[0], other, crossed[1]]

    def core_sum(kept, given, rounded):
        both = []
        for dz in range(2):
            crossed = receive(given[dz], sibling)
            summed = kept[dz].astype(f32) + crossed.astype(f32)
            both.append(summed.astype(bf16) if rounded[dz] else summed)
        return both

    def call(place, *args, **kwargs):
        parts = exchange_part(place, *args, **kwargs)
        return lax.optimization_barrier((place, *parts))

    coulombs = [
        coulomb_kernel(screening, (weights[a], weights[b])) for a, b in ((0, 0), (1, 1), (0, 1))
    ]
    *coulombs, halves[0][1], halves[1][1] = lax.optimization_barrier(
        (*coulombs, halves[0][1], halves[1][1])
    )
    two = pieces(0) + pieces(1)
    place, *earlier = call(
        place, two + [first], coulombs[0], matrices, two_targets=True, stage="first"
    )
    mark = place
    _, sent = lax.optimization_barrier((mark, own))
    halves[3][1] = receive(sent, offset_source(0, 0, 1, 0))
    place, kept, given = call(place, two + [second], coulombs[1], matrices, True, "last", earlier)
    crossed = receive(given, sibling)
    summed = (kept.astype(f32) + crossed.astype(f32)).astype(bf16)
    sums = [[summed[n, dz] for dz in range(2)] for n in range(2)]
    place, *flat = lax.optimization_barrier((place, *sums[0], *sums[1]))
    sums[:2] = [flat[:2], flat[2:]]
    place, kept, given = call(place, pieces(2, mark) + [first, second], coulombs[2], matrices)
    sums.append(core_sum(kept[0], given[0], (True, True)))
    place, *sums[2] = lax.optimization_barrier((place, *sums[2]))
    place, kept, given = call(place, pieces(3, mark) + [first, second], coulombs[2], matrices)
    crossed = receive(given[0, 1], sibling)
    crossed_0 = receive(given[0, 0], sibling)
    leaving = (kept[0, 1].astype(f32) + crossed.astype(f32)).astype(bf16)
    leaving, kept_0 = lax.optimization_barrier((leaving, kept[0, 0]))
    sums.append([kept_0.astype(f32) + crossed_0.astype(f32), leaving])
    arrived = {}
    for n, ((dy, dx), both) in enumerate(zip(orders, sums)):
        for dz in range(2):
            if (dy, dx, dz) != (0, 0, 0):
                arrived[n, dz] = receive(both[dz], offset_source(dy, dx, dz, 0)).astype(f32)
    early = sum((arrived[n, dz] for n in range(3) for dz in range(2)), sums[3][0])
    early = lax.optimization_barrier(early)
    return -(early + arrived[3, 1])[None]


def solution(mesh):
    in_specs = (P("tgt", "grp", None, None), P("tgt", None, None, None), P(), P(), P())
    out_specs = P("tgt", "grp", None, None)

    return jax.shard_map(body, mesh=mesh, in_specs=in_specs, out_specs=out_specs, check_vma=False)
```
